32 devices in a mesh: shard: 4 (over y, x), rep: 8 (over z, core).
Axes of the slice: x: 2, y: 2, z: 4, core: 2. Of those that a mesh axis runs over, the one named last changes fastest.
Arguments:
- tokens: bfloat16 [16384, 8192], P('rep', 'shard'), may hold values from -21 to 21
- key_cotangent: bfloat16 [16384, 1024], P('rep'), may hold values from -21 to 21
- value_cotangent: bfloat16 [16384, 1024], P('rep'), may hold values from -21 to 21
- key_weight: float32 [8192, 1024], P(('shard', 'rep')), may hold values from -0.75 to 0.75
- value_weight: float32 [8192, 1024], P(('shard', 'rep')), may hold values from -0.75 to 0.75
- key_moment: float32 [8192, 1024], P(('shard', 'rep')), may hold values from -6 to 6
- value_moment: float32 [8192, 1024], P(('shard', 'rep')), may hold values from -6 to 6
Outputs:
- new_key_weight: float32 [8192, 1024], P(('shard', 'rep'))
- new_value_weight: float32 [8192, 1024], P(('shard', 'rep'))
- new_key_moment: float32 [8192, 1024], P(('shard', 'rep'))
- new_value_moment: float32 [8192, 1024], P(('shard', 'rep'))
The draws below stay inside these ranges and needn't reach their ends.
All inputs are finite; a program needn't handle non-finite values.
Results may differ from the reference program's by a relative error of at most 0.0003.
Values may be sent and summed in bfloat16 or wider, within the bound.
A program may use at most 128 MiB of HBM per device.

```python
import math
import jax
import jax.numpy as jnp
from jax import lax

D = 8192
KV = 1024
TOK_DEV = 2048
TOKENS = 16384
N_REP = 8


def shifted_draw(key, columns, column_scale):
    shift_key, noise_key = jax.random.split(key, 2)
    shift_size = 1.22 * TOK_DEV ** (-0.25)
    shifted = jnp.clip(jax.random.normal(shift_key, (columns,), jnp.float32), -4.0, 4.0) * shift_size
    jitter = jnp.clip(jax.random.normal(noise_key, (TOKENS, columns), jnp.float32), -4.0, 4.0)
    return (column_scale[None, :] * (shifted[None, :] + jitter)).astype(jnp.bfloat16)


def draw_tokens(key, part):
    folded = jax.random.fold_in(key, 11)
    position_ramp = jnp.arange(D, dtype=jnp.float32) / (D - 1)
    column_scale = 3.0 ** position_ramp
    return shifted_draw(folded, D, column_scale)


def cotangent_draw(key, salt_value):
    folded = jax.random.fold_in(key, salt_value)
    scale_key, remaining = jax.random.split(folded, 2)
    column_scale = jnp.exp(jax.random.uniform(scale_key, (KV,), jnp.float32, math.log(0.3), math.log(3.0)))
    return shifted_draw(remaining, KV, column_scale)


def draw_key_cotangent(key, part):
    return cotangent_draw(key, 23)


def draw_value_cotangent(key, part):
    return cotangent_draw(key, 37)


def block_levels(rng, dims, cuts, least, top_value):
    def one(position, blocks):
        draws = jax.random.uniform(jax.random.fold_in(jax.random.fold_in(rng, 6), position), (blocks,), jnp.float32, least / len(cuts), top_value / len(cuts))
        return jnp.repeat(jnp.exp(draws), dims[position] // blocks).reshape((-1,) + (1,) * (len(dims) - position - 1))

    factor_of = one(*cuts[0])
    for cut in cuts[1:]:
        factor_of = factor_of * one(*cut)
    return factor_of


def normal_values(rng, shape, deviation, reach, cuts=(), kind=jnp.bfloat16):
    result = deviation * jax.random.normal(rng, shape, jnp.float32)
    if cuts:
        result = result * block_levels(rng, shape, cuts, -0.22, 0.18)
    return jnp.clip(result, -reach, reach).astype(kind)


def setup_inputs(seed: int = 0) -> dict:
    seeds = jax.random.split(jax.random.key(seed), 8)
    return {
        "tokens": draw_tokens(jax.random.fold_in(seeds[7], 71), 0),
        "key_cotangent": draw_key_cotangent(jax.random.fold_in(seeds[7], 71), 0),
        "value_cotangent": draw_value_cotangent(jax.random.fold_in(seeds[7], 71), 0),
        "key_weight": normal_values(seeds[3], (D, KV), 0.05, 0.75, ((0, 32),), jnp.float32),
        "value_weight": normal_values(seeds[4], (D, KV), 0.05, 0.75, ((0, 32),), jnp.float32),
        "key_moment": normal_values(seeds[5], (D, KV), 1.0, 6.0, ((0, 32),), jnp.float32),
        "value_moment": normal_values(seeds[6], (D, KV), 1.0, 6.0, ((0, 32),), jnp.float32),
    }


EPSILON = 1e-06
MOMENTUM_DECAY = 0.9
STEP_SIZE = 0.01

def replica_grad(tokens, cotangent, replica):
    token_rows = tokens[replica * TOK_DEV:(replica + 1) * TOK_DEV]
    cotangent_rows = cotangent[replica * TOK_DEV:(replica + 1) * TOK_DEV]
    product = lax.dot_general(token_rows, cotangent_rows, (((0,), (0,)), ((), ())), preferred_element_type=jnp.float32)
    return product * (1.0 / math.sqrt(TOK_DEV))

def combine(left_part, right_part):
    cross = jnp.sum(left_part * right_part)
    left_square = jnp.sum(left_part * left_part)
    right_square = jnp.sum(right_part * right_part)
    left_coef = 1.0 - cross / (2.0 * (left_square + EPSILON))
    right_coef = 1.0 - cross / (2.0 * (right_square + EPSILON))
    return left_coef * left_part + right_coef * right_part

def merged_tree(tokens, cotangent, start_index, members):
    if members == 1:
        return replica_grad(tokens, cotangent, start_index)
    half_members = members // 2
    left_part = merged_tree(tokens, cotangent, start_index, half_members)
    right_part = merged_tree(tokens, cotangent, start_index + half_members, half_members)
    return combine(left_part, right_part)

def reference(tokens, key_cotangent, value_cotangent, key_weight, value_weight, key_moment, value_moment):
    key_merged = merged_tree(tokens, key_cotangent, 0, N_REP)
    value_merged = merged_tree(tokens, value_cotangent, 0, N_REP)
    new_key_moment = MOMENTUM_DECAY * key_moment + key_merged
    new_value_moment = MOMENTUM_DECAY * value_moment + value_merged
    new_key_weight = key_weight - STEP_SIZE * new_key_moment
    new_value_weight = value_weight - STEP_SIZE * new_value_moment
    return (new_key_weight, new_value_weight, new_key_moment, new_value_moment)
```

```python
import functools
import math

import jax
import jax.numpy as jnp
from jax import lax
from jax.experimental import pallas as pl
from jax.experimental.pallas import tpu as pltpu
from jax.sharding import PartitionSpec as P

EPSILON = 1e-06
MOMENTUM_DECAY = 0.9
STEP_SIZE = 0.01
TINY_BOUND = 1e-16
TOP = 32768.0
FLOOR = 2.0**-120
CODE = jnp.bfloat16
MESH = pl.DeviceIdType.MESH
LANES = 128
ROWS = 16
PARTS = 4


def pair_coefs(cross, first_square, second_square):
    first = 1.0 - cross / (2.0 * (first_square + EPSILON))
    second = 1.0 - cross / (2.0 * (second_square + EPSILON))
    return first, second


def tree_coefs(gram):
    count = len(gram)
    coefs = [1.0] * count
    span = 1
    while len(gram) > 1:
        pairs = [
            pair_coefs(gram[i][i + 1], gram[i][i], gram[i + 1][i + 1])
            for i in range(0, len(gram), 2)
        ]
        for member in range(count):
            coefs[member] = coefs[member] * pairs[member // (2 * span)][member // span % 2]
        half = len(gram) // 2
        merged = [[None] * half for _ in range(half)]
        for i in range(half):
            for j in range(half):
                merged[i][j] = sum(
                    pairs[i][a] * pairs[j][b] * gram[2 * i + a][2 * j + b]
                    for a in range(2)
                    for b in range(2)
                )
        gram = merged
        span *= 2
    return coefs


def norm_bound(coefs, squares):
    bound = jnp.abs(coefs[0]) * jnp.sqrt(squares[0]) + jnp.abs(coefs[1]) * jnp.sqrt(squares[1])
    return jnp.maximum(bound, TINY_BOUND)


def sided(is_first, own, other):
    return jnp.where(is_first, own, other), jnp.where(is_first, other, own)


def encode(value):
    power = value * value
    power = power * power
    power = power * power
    return jnp.where(value < 0.0, -power, power).astype(CODE)


def decode(coded):
    coded = coded.astype(jnp.float32)
    fourth = lax.rsqrt(lax.rsqrt(jnp.maximum(jnp.abs(coded), FLOOR)))
    eighth = fourth * lax.rsqrt(fourth)
    return jnp.where(coded > 0.0, eighth, jnp.where(coded < 0.0, -eighth, 0.0))


def fold(product):
    total = jnp.sum(product.reshape(-1, 8, product.shape[-1]), axis=0)
    return sum(total[:, i : i + LANES] for i in range(0, total.shape[1], LANES))


def scalar(tile):
    return jnp.sum(jnp.sum(tile, axis=0, keepdims=True), axis=1, keepdims=True)


class Exchange:
    def __init__(self, span, shard_count, rep, shard, payload, inbox, send_sem, recv_sem):
        self.span, self.shard_count, self.rep, self.shard = span, shard_count, rep, shard
        self.payload, self.inbox = payload, inbox
        self.send_sem, self.recv_sem = send_sem, recv_sem
        self.shape = payload.shape

    def copy(self, slot):
        inside = lax.rem(self.rep, self.span)
        near, far = lax.rem(slot, self.span), lax.div(slot, self.span)
        target = self.rep - inside + lax.rem(inside + near, self.span)
        return pltpu.make_async_remote_copy(
            src_ref=self.payload,
            dst_ref=self.inbox.at[slot],
            send_sem=self.send_sem.at[slot],
            recv_sem=self.recv_sem.at[slot],
            device_id=(lax.rem(self.shard + far, self.shard_count), target),
            device_id_type=MESH,
        )

    def start(self, placed):
        flat = lax.broadcasted_iota(jnp.int32, self.shape, 0) * LANES
        flat = flat + lax.broadcasted_iota(jnp.int32, self.shape, 1)
        tile = jnp.zeros(self.shape, jnp.float32)
        for place, value in placed:
            tile = jnp.where(flat == place, value, tile)
        self.payload[...] = tile

        @pl.loop(1, self.span * self.shard_count)
        def _(slot):
            self.copy(slot).start()

    def finish(self):
        @pl.loop(1, self.span * self.shard_count)
        def _(slot):
            self.copy(slot).wait()

        total = self.payload[...]
        for slot in range(1, self.span * self.shard_count):
            total = total + self.inbox[slot]
        return lambda place: total[
            place // LANES : place // LANES + 1, place % LANES : place % LANES + 1
        ]


def owns(rep, shard, members):
    return (shard == 0) & (lax.rem(rep, members) == 0)


def final_places(sums, count, size, base, scale, rep, shard):
    unit = lax.div(rep, size)
    for (i, j), value in sums:
        left = lax.rem(unit - i + count, count)
        right = lax.rem(unit - j + count, count)
        yield base + jnp.minimum(left, right) * count + jnp.maximum(left, right), value
    yield base + count * count + unit, jnp.where(owns(rep, shard, size), scale, 0.0)


def final_weights(read, count, size, base, rep):
    unit = lax.div(rep, size)
    scales = [read(base + count * count + i) for i in range(count)]
    gram = [[None] * count for _ in range(count)]
    for i in range(count):
        for j in range(i, count):
            gram[i][j] = read(base + i * count + j) * (scales[i] * scales[j])
            gram[j][i] = gram[i][j]
    weights = [coef * scale for coef, scale in zip(tree_coefs(gram), scales)]
    for step in range(count):
        source = lax.rem(unit - step + count, count)
        chosen = weights[0]
        for i in range(1, count):
            chosen = jnp.where(source == i, weights[i], chosen)
        yield chosen


def merge_kernel(replicas, shard_count, *refs):
    (tokens_hbm, key_hbm, value_hbm, params_hbm) = refs[0], refs[1], refs[2], refs[3:7]
    outs = refs[7:11]
    (
        tokens, cotangents, key_full, value_full, key_other, value_other,
        key_send, key_recv, half_send, half_recv, last_send, last_recv,
        params, held,
        key_pay, key_in, value_pay, value_in, duo_pay, duo_in, final_pay, final_in,
        token_sem, load_sem, swap_send, swap_recv,
        key_ss, key_rs, half_ss, half_rs, last_ss, last_rs,
        kx_s, kx_r, vx_s, vx_r, dx_s, dx_r, fx_s, fx_r,
    ) = refs[11:]
    rep, shard = lax.axis_index("rep"), lax.axis_index("shard")
    groups, duos = replicas // 2, replicas // 4
    core, group = lax.rem(rep, 2), lax.div(rep, 2)
    half, duo = lax.rem(group, 2), lax.div(group, 2)
    block, features = key_other.shape[1], key_other.shape[2]
    factor = 1.0 / math.sqrt(tokens.shape[0])
    barrier = pltpu.get_barrier_semaphore()

    @pl.loop(1, replicas * shard_count)
    def _(slot):
        peer = (
            lax.rem(shard + lax.div(slot, replicas), shard_count),
            lax.rem(rep + lax.rem(slot, replicas), replicas),
        )
        pl.semaphore_signal(barrier, inc=1, device_id=peer, device_id_type=MESH)

    def remote(source, target, send_sem, recv_sem, peer):
        return pltpu.make_async_remote_copy(
            src_ref=source, dst_ref=target, send_sem=send_sem, recv_sem=recv_sem,
            device_id=(shard, peer), device_id_type=MESH,
        )

    unit = 2 * block

    def token_copy(j):
        columns = pl.ds(pl.multiple_of(j * unit, unit), unit)
        return pltpu.make_async_copy(
            tokens_hbm.at[:, columns], tokens.at[:, columns], token_sem.at[j]
        )

    loads = [
        pltpu.make_async_copy(key_hbm, cotangents.at[0], load_sem.at[0]),
        pltpu.make_async_copy(value_hbm, cotangents.at[1], load_sem.at[1]),
    ]
    loads += [
        pltpu.make_async_copy(source, params.at[i], load_sem.at[2 + i])
        for i, source in enumerate(params_hbm)
    ]
    loads[0].start()
    for j in range(groups):
        token_copy(j).start()
    for load in loads[1:]:
        load.start()

    def swap(which, j):
        full, other = (key_full, key_other) if which == 0 else (value_full, value_other)
        return remote(
            full.at[j, 1 - core], other.at[j], swap_send.at[which, j], swap_recv.at[which, j],
            rep + 1 - 2 * core,
        )

    def multiply(which, j):
        full = key_full if which == 0 else value_full
        left = tokens[:, pl.ds(pl.multiple_of(j * unit, unit), unit)]
        width = min(features, 512)
        for at in range(0, features, width):
            product = lax.dot_general(
                left, cotangents[which, :, at : at + width], (((0,), (0,)), ((), ())),
                preferred_element_type=jnp.float32,
            ) * factor
            full[j, 0, :, at : at + width] = product[:block]
            full[j, 1, :, at : at + width] = product[block:]

    def rows(i, size=ROWS):
        return pl.ds(pl.multiple_of(i * size, size), size)

    zero = jnp.zeros((8, LANES), jnp.float32)

    def duel(pairs, sums):
        for own, other in pairs:
            def body(i, carry, own=own, other=other):
                left, right = own(rows(i)), other(rows(i))
                cross, first, second = carry
                return (
                    cross + fold(left * right),
                    first + fold(left * left),
                    second + fold(right * right),
                )
            sums = lax.fori_loop(0, block // ROWS, body, sums)
        return sums

    def pair_sums(which):
        full, other = (key_full, key_other) if which == 0 else (value_full, value_other)

        def body(j, sums):
            swap(which, j).wait_recv()
            return duel([(lambda r: full[j, core, r, :], lambda r: other[j, r, :])], sums)

        return [scalar(tile) for tile in lax.fori_loop(0, groups, body, (zero,) * 3)]

    def pair_places(sums, is_first):
        first, second = sided(is_first, sums[1], sums[2])
        return [(0, sums[0]), (1, first), (2, second)]

    def pair_finish(read):
        squares = (read(1), read(2))
        first, second = pair_coefs(read(0), *squares)
        scale = norm_bound((first, second), squares) / TOP
        own, other = sided(core == 0, first / scale, second / scale)
        return own, other, scale

    def hold(at, values):
        for i, value in enumerate(values):
            held[at + i : at + i + 1, :] = jnp.broadcast_to(value, (1, LANES))

    def holds(at, count):
        return [held[at + i : at + i + 1, 0:1] for i in range(count)]

    def around(span, *scratch):
        return Exchange(span, shard_count, rep, shard, *scratch)

    key_exchange = around(2, key_pay, key_in, kx_s, kx_r)
    value_exchange = around(2, value_pay, value_in, vx_s, vx_r)
    duo_exchange = around(4, duo_pay, duo_in, dx_s, dx_r)
    final_exchange = around(replicas, final_pay, final_in, fx_s, fx_r)

    part = block // PARTS

    def key_copy(step, q):
        target = lax.rem(group + step, groups)
        place = pl.ds(q * part, part)
        return remote(
            key_send.at[step - 1, place], key_recv.at[step - 1, place],
            key_ss.at[step - 1, q], key_rs.at[step - 1, q], 2 * target + core,
        )

    def key_encode(step):
        own, other = holds(0, 2)
        target = lax.rem(group + step, groups)

        @pl.loop(0, block // ROWS)
        def _(i):
            r = rows(i)
            key_send[step - 1, r, :] = encode(
                own * key_full[target, core, r, :] + other * key_other[target, r, :]
            )

    def half_copy(d):
        return remote(
            half_send.at[d], half_recv.at[d], half_ss.at[d], half_rs.at[d],
            rep + 2 - 4 * half,
        )

    def last_copy(step):
        target = lax.rem(duo + step, duos)
        return remote(
            last_send.at[step - 1], last_recv.at[step - 1],
            last_ss.at[step - 1], last_rs.at[step - 1], rep + 4 * (target - duo),
        )

    first_steps = [groups - 1]
    last_steps = [1]
    middle_steps = list(range(groups - 2, 1, -1))

    @pl.loop(0, groups)
    def _(j):
        token_copy(j).wait()

        @pl.when(j == 0)
        def _():
            loads[0].wait()

        multiply(0, j)

        @pl.when(j == 0)
        def _():
            pl.semaphore_wait(barrier, replicas * shard_count - 1)

        swap(0, j).start()

    key_exchange.start(pair_places(pair_sums(0), core == 0))
    loads[1].wait()

    @pl.loop(0, groups)
    def _(j):
        @pl.when(j == 1)
        def _():
            hold(0, pair_finish(key_exchange.finish()))
            for step in first_steps:
                key_encode(step)
                for q in range(PARTS):
                    key_copy(step, q).start()
            for step in middle_steps + last_steps:
                key_encode(step)
            key_copy(1, 0).start()

        multiply(1, j)
        swap(1, j).start()

    value_exchange.start(pair_places(pair_sums(1), core == 0))

    key_blocks = key_other
    own, other, key_scale = holds(0, 3)

    @pl.loop(0, block // ROWS)
    def _(i):
        r = rows(i)
        key_blocks[0, r, :] = own * key_full[group, core, r, :] + other * key_other[group, r, :]

    own, other, value_scale = pair_finish(value_exchange.finish())
    hold(3, (own, other, value_scale))
    for d in range(duos):
        @pl.loop(0, block // ROWS)
        def _(i):
            r, j = rows(i), 2 * d + 1 - half
            half_send[d, r, :] = encode(
                own * value_full[j, core, r, :] + other * value_other[j, r, :]
            )

        half_copy(d).start()
    for step in middle_steps:
        key_copy(step, 0).start()
    own, other = holds(3, 2)
    for d in range(duos):
        @pl.loop(0, block // ROWS)
        def _(i):
            r, j = rows(i), 2 * d + half
            value_other[j, r, :] = own * value_full[j, core, r, :] + other * value_other[j, r, :]

    def absorb(read, blocks, slot, ready, sums, begin, size):
        mine = sorted(ready) + [slot]

        def body(i, carry):
            r = rows(i)
            value = read(r)
            blocks(slot, r, value)
            others = [blocks(b, r) for b in mine[:-1]] + [value]
            return tuple(c + fold(value * o) for c, o in zip(carry, others))

        stop = (begin + size) // ROWS
        start = tuple(
            sums.get((min(slot, b), max(slot, b)), zero) for b in mine
        )
        done = lax.fori_loop(begin // ROWS, stop, body, start)
        for b, tile in zip(mine, done):
            sums[(min(slot, b), max(slot, b))] = tile

    def key_access(slot, r, value=None):
        if value is None:
            return key_blocks[slot, r, :]
        key_blocks[slot, r, :] = value

    def value_access(slot, r, value=None):
        if value is None:
            return value_full[slot, 0, r, :]
        value_full[slot, 0, r, :] = value

    key_sums, value_sums, key_ready, value_ready = {}, {}, [], []

    def absorb_own_key():
        def body(i, carry):
            value = key_blocks[0, rows(i), :]
            return carry + fold(value * value)
        key_sums[(0, 0)] = lax.fori_loop(0, block // ROWS, body, zero)
        key_ready.append(0)

    def absorb_key(step):
        for q in range(PARTS):
            key_copy(step, q).wait_recv()
            absorb(
                lambda r: decode(key_recv[step - 1, r, :]), key_access, step, key_ready,
                key_sums, q * part, part,
            )
        key_ready.append(step)

    absorb_own_key()
    for step in first_steps:
        absorb_key(step)

    for d in range(duos):
        half_copy(d).wait_recv()

        def body(i, carry, d=d):
            r = rows(i)
            left = value_other[2 * d + half, r, :]
            right = decode(half_recv[d, r, :])
            value_other[2 * d + 1 - half, r, :] = right
            cross, first, second = carry
            return (
                cross + fold(left * right),
                first + fold(left * left),
                second + fold(right * right),
            )

        duo_sums = lax.fori_loop(
            0, block // ROWS, body, (zero,) * 3 if d == 0 else duo_sums
        )
    even = half == 0
    places = pair_places([scalar(tile) for tile in duo_sums], even)
    mine = jnp.where(owns(rep, shard, 2), value_scale, 0.0)
    low, high = sided(even, mine, jnp.zeros_like(mine))
    duo_exchange.start(places + [(3, low), (4, high)])
    for step in middle_steps:
        for q in range(1, PARTS):
            key_copy(step, q).start()
    for j in range(groups):
        swap(1, j).wait_send()
    read = duo_exchange.finish()
    low, high = read(3), read(4)
    squares = (read(1) * (low * low), read(2) * (high * high))
    first, second = pair_coefs(read(0) * (low * high), *squares)
    duo_scale = norm_bound((first, second), squares) / TOP
    own, other = sided(even, first * low / duo_scale, second * high / duo_scale)

    def duo_block(target, r):
        return (
            own * value_other[2 * target + half, r, :]
            + other * value_other[2 * target + 1 - half, r, :]
        )

    for step in range(1, duos):
        @pl.loop(0, block // ROWS)
        def _(i):
            r = rows(i)
            last_send[step - 1, r, :] = encode(duo_block(lax.rem(duo + step, duos), r))

        last_copy(step).start()
    for step in last_steps:
        for q in range(1, PARTS):
            key_copy(step, q).start()
    absorb(
        lambda r: duo_block(duo, r), value_access, 0, value_ready, value_sums, 0, block
    )
    value_ready.append(0)
    for step in middle_steps:
        absorb_key(step)
    for step in range(1, duos):
        last_copy(step).wait_recv()
        absorb(
            lambda r: decode(last_recv[step - 1, r, :]), value_access, step, value_ready,
            value_sums, 0, block,
        )
        value_ready.append(step)
    for step in last_steps:
        absorb_key(step)

    key_base, value_base = 0, groups * (groups + 1)
    key_places = [(pair, scalar(tile)) for pair, tile in key_sums.items()]
    value_places = [(pair, scalar(tile)) for pair, tile in value_sums.items()]
    places = list(final_places(key_places, groups, 2, key_base, key_scale, rep, shard))
    places += list(final_places(value_places, duos, 4, value_base, duo_scale, rep, shard))
    final_exchange.start(places)
    for j in range(groups):
        swap(0, j).wait_send()
    for step in range(1, groups):
        for q in range(PARTS):
            key_copy(step, q).wait_send()
    for d in range(duos):
        half_copy(d).wait_send()
    for step in range(1, duos):
        last_copy(step).wait_send()
    for load in loads[2:]:
        load.wait()
    read = final_exchange.finish()
    key_weights = list(final_weights(read, groups, 2, key_base, rep))
    value_weights = list(final_weights(read, duos, 4, value_base, rep))

    @pl.loop(0, block // 8)
    def _(i):
        r = rows(i, 8)
        key_merged = sum(w * key_blocks[b, r, :] for b, w in enumerate(key_weights))
        value_merged = sum(w * value_full[b, 0, r, :] for b, w in enumerate(value_weights))
        for which, merged in enumerate((key_merged, value_merged)):
            moment = MOMENTUM_DECAY * params[2 + which, r, :] + merged
            outs[2 + which][r, :] = moment
            outs[which][r, :] = params[which, r, :] - STEP_SIZE * moment


def shards(
    tokens, key_cotangent, value_cotangent, key_weight, value_weight, key_moment, value_moment
):
    replicas, shard_count = lax.axis_size("rep"), lax.axis_size("shard")
    depth, width = tokens.shape
    features = key_cotangent.shape[1]
    groups, duos = replicas // 2, replicas // 4
    block = width // replicas
    f32, dma = jnp.float32, pltpu.SemaphoreType.DMA
    entries = groups * (groups + 1) + duos * (duos + 1)
    lines = -(-entries // LANES)

    def small(span, lines=1):
        return [
            pltpu.VMEM((lines, LANES), f32),
            pltpu.VMEM((span * shard_count, lines, LANES), f32),
        ]

    def coded(count):
        return [pltpu.VMEM((max(count, 1), block, features), CODE)] * 2

    def pair(*shape):
        return [dma(shape)] * 2

    scratch = [
        pltpu.VMEM((depth, width), tokens.dtype),
        pltpu.VMEM((2, depth, features), key_cotangent.dtype),
        pltpu.VMEM((groups, 2, block, features), f32),
        pltpu.VMEM((groups, 2, block, features), f32),
        pltpu.VMEM((groups, block, features), f32),
        pltpu.VMEM((groups, block, features), f32),
        *coded(groups - 1), *coded(duos), *coded(duos - 1),
        pltpu.VMEM((4, block, features), f32),
        pltpu.VMEM((8, LANES), f32),
        *small(2), *small(2), *small(4), *small(replicas, lines),
        dma((groups,)), dma((6,)), *pair(2, groups),
        *pair(groups - 1, PARTS), *pair(duos), *pair(max(duos - 1, 1)),
        *pair(2 * shard_count), *pair(2 * shard_count), *pair(4 * shard_count),
        *pair(replicas * shard_count),
    ]
    row = jax.ShapeDtypeStruct((block, features), f32)
    return pl.pallas_call(
        functools.partial(merge_kernel, replicas, shard_count),
        out_shape=[row] * 4,
        in_specs=[pl.BlockSpec(memory_space=pl.ANY)] * 7,
        out_specs=[pl.BlockSpec(memory_space=pltpu.VMEM)] * 4,
        scratch_shapes=scratch,
        compiler_params=pltpu.CompilerParams(
            collective_id=0, has_side_effects=True, vmem_limit_bytes=62 * 2**20
        ),
    )(
        tokens, key_cotangent, value_cotangent, key_weight, value_weight, key_moment, value_moment
    )


def solution(mesh):
    grads = (P("rep", None),) * 2
    rows = (P(("shard", "rep"), None),) * 4
    return jax.shard_map(
        shards, mesh=mesh, in_specs=(P("rep", "shard"),) + grads + rows, out_specs=rows,
        check_vma=False,
    )
```

```python
import functools
import math

import jax
import jax.numpy as jnp
from jax import lax
from jax.experimental import pallas as pl
from jax.experimental.pallas import tpu as pltpu
from jax.sharding import PartitionSpec as P

EPSILON = 1e-06
MOMENTUM_DECAY = 0.9
STEP_SIZE = 0.01
TINY_BOUND = 1e-16
TOP = 32768.0
FLOOR = 2.0**-120
CODE = jnp.bfloat16
MESH = pl.DeviceIdType.MESH
LANES = 128
ROWS = 32
PARTS = 4
BUNCHES = 4
SPLITS = 2
EARLY = 0
BEHIND = 3
RAW = 2
VMEM_LIMIT = 54 * 2**20


def pair_coefs(cross, first_square, second_square):
    first = 1.0 - cross / (2.0 * (first_square + EPSILON))
    second = 1.0 - cross / (2.0 * (second_square + EPSILON))
    return first, second


def tree_coefs(gram):
    count = len(gram)
    coefs = [1.0] * count
    span = 1
    while len(gram) > 1:
        pairs = [
            pair_coefs(gram[i][i + 1], gram[i][i], gram[i + 1][i + 1])
            for i in range(0, len(gram), 2)
        ]
        for member in range(count):
            coefs[member] = coefs[member] * pairs[member // (2 * span)][member // span % 2]
        half = len(gram) // 2
        merged = [[None] * half for _ in range(half)]
        for i in range(half):
            for j in range(half):
                merged[i][j] = sum(
                    pairs[i][a] * pairs[j][b] * gram[2 * i + a][2 * j + b]
                    for a in range(2)
                    for b in range(2)
                )
        gram = merged
        span *= 2
    return coefs


def norm_bound(coefs, squares):
    bound = jnp.abs(coefs[0]) * jnp.sqrt(squares[0]) + jnp.abs(coefs[1]) * jnp.sqrt(squares[1])
    return jnp.maximum(bound, TINY_BOUND)


def sided(is_first, own, other):
    return jnp.where(is_first, own, other), jnp.where(is_first, other, own)


def encode(value):
    power = value * value
    power = power * power
    power = power * power
    return jnp.where(value < 0.0, -power, power).astype(CODE)


def decode(coded):
    coded = coded.astype(jnp.float32)
    fourth = lax.rsqrt(lax.rsqrt(jnp.maximum(jnp.abs(coded), FLOOR)))
    eighth = fourth * lax.rsqrt(fourth)
    return jnp.where(coded > 0.0, eighth, jnp.where(coded < 0.0, -eighth, 0.0))


def tree_sum(terms):
    while len(terms) > 1:
        terms = [sum(terms[i : i + 2]) for i in range(0, len(terms), 2)]
    return terms[0]


def fold(product):
    return tree_sum([
        product[i : i + 8, j : j + LANES]
        for i in range(0, product.shape[0], 8)
        for j in range(0, product.shape[1], LANES)
    ])


def scalar(tile):
    return jnp.sum(jnp.sum(tile, axis=0, keepdims=True), axis=1, keepdims=True)


class Exchange:
    def __init__(self, span, shard_count, rep, shard, payload, inbox, send_sem, recv_sem):
        self.span, self.shard_count, self.rep, self.shard = span, shard_count, rep, shard
        self.payload, self.inbox = payload, inbox
        self.send_sem, self.recv_sem = send_sem, recv_sem
        self.shape = payload.shape

    def copy(self, slot):
        inside = lax.rem(self.rep, self.span)
        near, far = lax.rem(slot, self.span), lax.div(slot, self.span)
        target = self.rep - inside + lax.rem(inside + near, self.span)
        return pltpu.make_async_remote_copy(
            src_ref=self.payload,
            dst_ref=self.inbox.at[slot],
            send_sem=self.send_sem.at[slot],
            recv_sem=self.recv_sem.at[slot],
            device_id=(lax.rem(self.shard + far, self.shard_count), target),
            device_id_type=MESH,
        )

    def start(self, placed):
        flat = lax.broadcasted_iota(jnp.int32, self.shape, 0) * LANES
        flat = flat + lax.broadcasted_iota(jnp.int32, self.shape, 1)
        tile = jnp.zeros(self.shape, jnp.float32)
        for place, value in placed:
            tile = jnp.where(flat == place, value, tile)
        self.payload[...] = tile

        @pl.loop(1, self.span * self.shard_count)
        def _(slot):
            self.copy(slot).start()

    def finish(self):
        @pl.loop(1, self.span * self.shard_count)
        def _(slot):
            self.copy(slot).wait()

        total = self.payload[...]
        for slot in range(1, self.span * self.shard_count):
            total = total + self.inbox[slot]

        def read(place):
            line, lane = place // LANES, place % LANES
            row = total[line : line + 1, :]
            return (pltpu.roll(row, LANES - lane, 1) if lane else row)[:, :1]

        return read


def owns(rep, shard, members):
    return (shard == 0) & (lax.rem(rep, members) == 0)


def final_places(sums, count, size, base, scale, rep, shard, offset):
    unit = lax.div(rep, size)
    for (i, j), value in sums:
        left = lax.rem(unit - offset(i) + count, count)
        right = lax.rem(unit - offset(j) + count, count)
        yield base + jnp.minimum(left, right) * count + jnp.maximum(left, right), value
    yield base + count * count + unit, jnp.where(owns(rep, shard, size), scale, 0.0)


def final_weights(read, count, size, base, rep, offset):
    unit = lax.div(rep, size)
    scales = [read(base + count * count + i) for i in range(count)]
    gram = [[None] * count for _ in range(count)]
    for i in range(count):
        for j in range(i, count):
            gram[i][j] = read(base + i * count + j) * (scales[i] * scales[j])
            gram[j][i] = gram[i][j]
    weights = [coef * scale for coef, scale in zip(tree_coefs(gram), scales)]
    for slot in range(count):
        source = lax.rem(unit - offset(slot) + count, count)
        chosen = weights[0]
        for i in range(1, count):
            chosen = jnp.where(source == i, weights[i], chosen)
        yield chosen


def merge_kernel(replicas, shard_count, *refs):
    tokens_hbm, key_hbm, value_hbm = refs[:3]
    key_out, value_out = refs[3:5]
    (
        tokens, cotangents, key_full, value_full, key_other, value_other,
        key_send, key_recv, half_send, half_recv, last_send, last_recv, raw_send, raw_recv,
        held, wide, raw_pay, raw_in,
        key_pay, key_in, value_pay, value_in, duo_pay, duo_in, final_pay, final_in,
        token_sem, load_sem, swap_send, swap_recv,
        key_ss, key_rs, half_ss, half_rs, last_ss, last_rs, raw_ss, raw_rs, rw_s, rw_r,
        kx_s, kx_r, vx_s, vx_r, dx_s, dx_r, fx_s, fx_r,
    ) = refs[5:]
    rep, shard = lax.axis_index("rep"), lax.axis_index("shard")
    groups, duos = replicas // 2, replicas // 4
    core, group = lax.rem(rep, 2), lax.div(rep, 2)
    half, duo = lax.rem(group, 2), lax.div(group, 2)
    block, features = key_other.shape[1], key_other.shape[2]
    width = features // SPLITS
    factor = 1.0 / math.sqrt(tokens.shape[0])
    size = min(block, ROWS)
    parts = min(PARTS, block // 16)
    part = block // parts
    barrier = pltpu.get_barrier_semaphore()

    forward = group < duos
    inner = (half == 1) == forward
    outer = jnp.logical_not(inner)

    def key_shift(step):
        return jnp.where(forward, step, groups - step)

    raw_target = lax.rem(group + key_shift(RAW), groups)
    before = lax.rem(group + groups - RAW, groups)
    after = lax.rem(group + RAW, groups)
    raw_before = (before < duos) & (lax.rem(before, 2) == 1)
    raw_after = (after >= duos) & (lax.rem(after, 2) == 0)
    receiver = raw_before | raw_after
    plain = jnp.logical_not(receiver)

    bunch = groups // BUNCHES
    span = 2 * block * bunch

    def token_copy(j):
        columns = pl.ds(pl.multiple_of(j * span, span), span)
        return pltpu.make_async_copy(
            tokens_hbm.at[:, columns], tokens.at[:, columns], token_sem.at[j]
        )

    def load(which, split):
        source = key_hbm if which == 0 else value_hbm
        columns = pl.ds(split * width, width)
        return pltpu.make_async_copy(
            source.at[:, columns], cotangents.at[which, :, columns], load_sem.at[which, split]
        )

    first = jnp.where(inner, lax.div(raw_target, bunch), 0)

    def order(k):
        return lax.rem(first + k, BUNCHES)

    token_copy(order(0)).start()
    for split in range(SPLITS):
        load(0, split).start()

    @pl.loop(1, replicas * shard_count)
    def _(slot):
        peer = (
            lax.rem(shard + lax.div(slot, replicas), shard_count),
            lax.rem(rep + lax.rem(slot, replicas), replicas),
        )
        pl.semaphore_signal(barrier, inc=1, device_id=peer, device_id_type=MESH)

    def remote(source, target, send_sem, recv_sem, peer):
        return pltpu.make_async_remote_copy(
            src_ref=source, dst_ref=target, send_sem=send_sem, recv_sem=recv_sem,
            device_id=(shard, peer), device_id_type=MESH,
        )

    def tensor(which):
        return (key_full, key_other) if which == 0 else (value_full, value_other)

    def place(split):
        return pl.ds(split * width, width)

    def swap(which, at, split):
        full, other = tensor(which)
        these = pl.ds(at * bunch, bunch)
        return remote(
            full.at[these, 1 - core, :, place(split)], other.at[these, :, place(split)],
            swap_send.at[which, at, split], swap_recv.at[which, at, split], rep + 1 - 2 * core,
        )

    def multiply(which, at, split):
        full = tensor(which)[0]
        left = tokens[:, pl.ds(pl.multiple_of(at * span, span), span)]
        product = lax.dot_general(
            left, cotangents[which, :, place(split)], (((0,), (0,)), ((), ())),
            preferred_element_type=jnp.float32,
        ) * factor
        for j in range(bunch):
            for side in range(2):
                begin = (2 * j + side) * block
                full[at * bunch + j, side, :, place(split)] = product[begin : begin + block]

    def duel(left, right, sums):
        products = (left * right, left * left, right * right)
        return tuple(s + fold(p) for s, p in zip(sums, products))

    def swapped(which, at, split, sums):
        full, other = tensor(which)
        for j in range(bunch):
            sums = duel(
                full[at * bunch + j, core, :, place(split)], other[at * bunch + j, :, place(split)],
                sums,
            )
        return sums

    def rows(i, size=size):
        return pl.ds(pl.multiple_of(i * size, size), size)

    def over(begin, length, body, start=None):
        if start is None:
            lax.fori_loop(begin // size, (begin + length) // size, lambda i, _: body(rows(i)), None)
            return None
        return lax.fori_loop(
            begin // size, (begin + length) // size, lambda i, c: body(rows(i), c), start
        )

    zero = jnp.zeros((8, LANES), jnp.float32)

    def pair_sums(which, sums):
        for split in range(SPLITS):
            swap(which, order(BUNCHES - 1), split).wait_recv()
            sums = swapped(which, order(BUNCHES - 1), split, sums)
        return [scalar(tile) for tile in sums]

    def pair_places(sums, is_first):
        first, second = sided(is_first, sums[1], sums[2])
        return [(0, sums[0]), (1, first), (2, second)]

    def pair_finish(read):
        squares = (read(1), read(2))
        first, second = pair_coefs(read(0), *squares)
        scale = norm_bound((first, second), squares) / TOP
        own, other = sided(core == 0, first / scale, second / scale)
        return own, other, scale

    def hold(at, values):
        for i, value in enumerate(values):
            held[at + i : at + i + 1, :] = jnp.broadcast_to(value, (1, LANES))

    def holds(at, count):
        return [held[at + i : at + i + 1, 0:1] for i in range(count)]

    def around(span, *scratch):
        return Exchange(span, shard_count, rep, shard, *scratch)

    key_exchange = around(2, key_pay, key_in, kx_s, kx_r)
    value_exchange = around(2, value_pay, value_in, vx_s, vx_r)
    duo_exchange = around(4, duo_pay, duo_in, dx_s, dx_r)
    final_exchange = around(replicas, final_pay, final_in, fx_s, fx_r)

    def key_copy(step, q):
        shift = key_shift(step)
        place = pl.ds(q * part, part)
        return remote(
            key_send.at[shift - 1, place], key_recv.at[shift - 1, place],
            key_ss.at[shift - 1, q], key_rs.at[shift - 1, q],
            2 * lax.rem(group + shift, groups) + core,
        )

    def key_start(step, begin=0, end=parts):
        for q in range(begin, min(end, parts)):
            key_copy(step, q).start()

    def key_encode(step, q=None):
        own, other = holds(0, 2)
        shift = key_shift(step)
        target = lax.rem(group + shift, groups)

        def body(r):
            key_send[shift - 1, r, :] = encode(
                own * key_full[target, core, r, :] + other * key_other[target, r, :]
            )

        over(0 if q is None else q * part, block if q is None else part, body)

    def half_copy(d, q):
        place = pl.ds(q * part, part)
        return remote(
            half_send.at[d, place], half_recv.at[d, place], half_ss.at[d, q], half_rs.at[d, q],
            rep + 2 - 4 * half,
        )

    def last_copy(step, q):
        place = pl.ds(q * part, part)
        target = lax.rem(duo + step, duos)
        return remote(
            last_send.at[step - 1, place], last_recv.at[step - 1, place],
            last_ss.at[step - 1, q], last_rs.at[step - 1, q], rep + 4 * (target - duo),
        )

    far, near = groups - 1, 1
    middle = list(range(groups - 2, 1, -1))
    mixed = [step for step in middle if step != RAW]

    def advance(which, k, sums):
        for split in range(SPLITS):
            swap(which, order(k - 1), split).wait_recv()
            sums = swapped(which, order(k - 1), split, sums)
            multiply(which, order(k), split)
            swap(which, order(k), split).start()
        return sums

    token_copy(order(0)).wait()
    for split in range(SPLITS):
        load(0, split).wait()
        if split == 0:
            token_copy(order(1)).start()
        multiply(0, order(0), split)

    def raw_copy(side):
        return remote(
            raw_send.at[side], raw_recv.at[core], raw_ss.at[side], raw_rs.at[core],
            2 * raw_target + side,
        )

    def raw_weight(side):
        return remote(
            raw_pay.at[side], raw_in.at[core], rw_s.at[side], rw_r.at[core],
            2 * raw_target + side,
        )

    @pl.when(inner)
    def _():
        for side in range(2):
            def body(r, carry, side=side):
                value = key_full[raw_target, side, r, :]
                return carry + fold(value * value)

            square = scalar(over(0, block, body, zero))
            scale = jnp.maximum(jnp.sqrt(square), TINY_BOUND) / TOP
            hold(6 + side, [scale])
            inverse = 1.0 / scale

            def body(r, side=side):
                raw_send[side, r, :] = encode(inverse * key_full[raw_target, side, r, :])

            over(0, block, body)

    pl.semaphore_wait(barrier, replicas * shard_count - 1)
    for split in range(SPLITS):
        swap(0, order(0), split).start()

    @pl.when(inner)
    def _():
        for side in range(2):
            raw_copy(side).start()

    def body(k, sums):
        token_copy(order(k)).wait()

        @pl.when(k < BUNCHES - 1)
        def _():
            token_copy(order(k + 1)).start()

        @pl.when(k == BUNCHES - 1)
        def _():
            for split in range(SPLITS):
                load(1, split).start()

        return advance(0, k, sums)

    sums = lax.fori_loop(1, BUNCHES, body, (zero,) * 3)
    key_exchange.start(pair_places(pair_sums(0, sums), core == 0))
    for split in range(SPLITS):
        load(1, split).wait()
    for split in range(SPLITS):
        multiply(1, order(0), split)
        swap(1, order(0), split).start()

    hold(0, pair_finish(key_exchange.finish()))

    @pl.when(outer)
    def _():
        for q in range(parts):
            key_encode(far, q)
            key_start(far, q, q + 1)

    @pl.when(inner)
    def _():
        own = holds(0, 1)[0]
        for side in range(2):
            weight = own * holds(6 + side, 1)[0]
            raw_pay[side] = jnp.broadcast_to(weight, (1, LANES))
            raw_weight(side).start()
        key_encode(near)
        key_start(near)

    sums = lax.fori_loop(1, BUNCHES, lambda at, sums: advance(1, at, sums), (zero,) * 3)
    value_exchange.start(pair_places(pair_sums(1, sums), core == 0))

    @pl.when(outer)
    def _():
        for step in middle:
            key_encode(step)
            key_start(step, 0, EARLY)
        key_encode(near)

    @pl.when(inner)
    def _():
        for step in mixed:
            key_encode(step)
            key_start(step, 0, EARLY)
        key_encode(far)


    own, other, value_scale = pair_finish(value_exchange.finish())
    hold(3, (own, other, value_scale))

    def half_block(r, d, side):
        j = 2 * d + side
        return own * value_full[j, core, r, :] + other * value_other[j, r, :]

    for d in range(duos):
        for q in range(parts):
            def body(r):
                half_send[d, r, :] = encode(half_block(r, d, 1 - half))

            over(q * part, part, body)
            half_copy(d, q).start()

    @pl.when(outer)
    def _():
        for step in middle:
            key_start(step, EARLY, BEHIND)

    for d in range(duos):
        def body(r):
            value_other[2 * d + half, r, :] = half_block(r, d, half)

        over(0, block, body)

    key_blocks = key_other
    own, other, key_scale = holds(0, 3)

    def body(r, carry):
        value = own * key_full[group, core, r, :] + other * key_other[group, r, :]
        key_blocks[0, r, :] = value
        return carry + fold(value * value)

    key_sums, value_sums = {(0, 0): over(0, block, body, zero)}, {}
    key_ready, value_ready = [0], []

    def absorb(read, blocks, slot, ready, sums, begin, length):
        def body(r, carry):
            value = read(r)
            blocks(slot, r, value)
            others = [blocks(b, r) for b in ready] + [value]
            return tuple(c + fold(value * o) for c, o in zip(carry, others))

        pairs = [(b, slot) for b in ready] + [(slot, slot)]
        start = tuple(sums.get(pair, zero) for pair in pairs)
        sums.update(zip(pairs, over(begin, length, body, start)))

    def key_access(slot, r, value=None):
        if value is None:
            return key_blocks[slot, r, :]
        key_blocks[slot, r, :] = value

    def value_access(slot, r, value=None):
        if value is None:
            return value_full[slot, 0, r, :]
        value_full[slot, 0, r, :] = value

    def key_offset(u):
        return jnp.where(half == 0, u, lax.rem(groups - u, groups))

    def value_offset(u):
        return u

    def key_arrival(u, q):
        shift, place = key_offset(u), pl.ds(q * part, part)
        remote(
            key_send.at[shift - 1, place], key_recv.at[shift - 1, place],
            key_ss.at[shift - 1, q], key_rs.at[shift - 1, q], rep + 1 - 2 * core,
        ).wait_recv()

    def absorb_key(u, q):
        key_arrival(u, q)
        absorb(
            lambda r: decode(key_recv[key_offset(u) - 1, r, :]), key_access, u, key_ready,
            key_sums, q * part, part,
        )

    @pl.when(receiver)
    def _():
        for source in range(2):
            remote(
                raw_send.at[source], raw_recv.at[source], raw_ss.at[source], raw_rs.at[source],
                rep + 1 - 2 * core,
            ).wait_recv()
            remote(
                raw_pay.at[source], raw_in.at[source], rw_s.at[source], rw_r.at[source],
                rep + 1 - 2 * core,
            ).wait_recv()

        def body(r):
            key_blocks[groups - RAW, r, :] = sum(
                raw_in[source][:, :1] * decode(raw_recv[source, r, :]) for source in range(2)
            )

        over(0, block, body)

    for q in range(parts):
        absorb_key(1, q)
    key_ready.append(1)

    duo_sums = (zero,) * 3
    for d in range(duos):
        for q in range(parts):
            half_copy(d, q).wait_recv()

            def body(r, carry):
                left = value_other[2 * d + half, r, :]
                right = decode(half_recv[d, r, :])
                value_other[2 * d + 1 - half, r, :] = right
                return duel(left, right, carry)

            duo_sums = over(q * part, part, body, duo_sums)
    even = half == 0
    places = pair_places([scalar(tile) for tile in duo_sums], even)
    mine = jnp.where(owns(rep, shard, 2), value_scale, 0.0)
    low, high = sided(even, mine, jnp.zeros_like(mine))
    duo_exchange.start(places + [(3, low), (4, high)])

    @pl.when(outer)
    def _():
        for step in middle:
            key_start(step, BEHIND)

    @pl.when(inner)
    def _():
        for step in mixed:
            key_start(step, EARLY)
        key_start(far)

    for at in range(BUNCHES):
        for split in range(SPLITS):
            swap(1, at, split).wait_send()
    read = duo_exchange.finish()
    low, high = read(3), read(4)
    squares = (read(1) * (low * low), read(2) * (high * high))
    first, second = pair_coefs(read(0) * (low * high), *squares)
    duo_scale = norm_bound((first, second), squares) / TOP
    own, other = sided(even, first * low / duo_scale, second * high / duo_scale)

    def duo_block(target, r):
        return (
            own * value_other[2 * target + half, r, :]
            + other * value_other[2 * target + 1 - half, r, :]
        )

    for step in range(1, duos):
        for q in range(parts):
            def body(r):
                last_send[step - 1, r, :] = encode(duo_block(lax.rem(duo + step, duos), r))

            over(q * part, part, body)
            last_copy(step, q).start()

    @pl.when(outer)
    def _():
        key_start(near)

    absorb(lambda r: duo_block(duo, r), value_access, 0, value_ready, value_sums, 0, block)
    value_ready.append(0)
    for u in range(2, groups - 1):
        if u == groups - RAW:
            @pl.when(plain)
            def _():
                for q in range(parts):
                    key_arrival(u, q)

                    def body(r):
                        key_blocks[u, r, :] = decode(key_recv[key_offset(u) - 1, r, :])

                    over(q * part, part, body)

            absorb(
                lambda r: key_blocks[u, r, :], key_access, u, key_ready, key_sums, 0, block
            )
        else:
            for q in range(parts):
                absorb_key(u, q)
        key_ready.append(u)
    for step in range(1, duos):
        for q in range(parts):
            last_copy(step, q).wait_recv()
            absorb(
                lambda r: decode(last_recv[step - 1, r, :]), value_access, step, value_ready,
                value_sums, q * part, part,
            )
            if step == duos - 1:
                absorb_key(groups - 1, q)
        value_ready.append(step)

    key_base, value_base = 0, groups * (groups + 1)
    key_places = [(pair, scalar(tile)) for pair, tile in key_sums.items()]
    value_places = [(pair, scalar(tile)) for pair, tile in value_sums.items()]
    final_exchange.start(
        list(final_places(key_places, groups, 2, key_base, key_scale, rep, shard, key_offset))
        + list(
            final_places(value_places, duos, 4, value_base, duo_scale, rep, shard, value_offset)
        )
    )
    for at in range(BUNCHES):
        for split in range(SPLITS):
            swap(0, at, split).wait_send()
    for step in range(1, groups):
        def drain():
            for q in range(parts):
                key_copy(step, q).wait_send()

        if step == RAW:
            pl.when(outer)(drain)
        else:
            drain()

    @pl.when(inner)
    def _():
        for side in range(2):
            raw_copy(side).wait_send()
            raw_weight(side).wait_send()

    for q in range(parts):
        for d in range(duos):
            half_copy(d, q).wait_send()
        for step in range(1, duos):
            last_copy(step, q).wait_send()
    read = final_exchange.finish()
    key_weights = list(final_weights(read, groups, 2, key_base, rep, key_offset))
    value_weights = list(final_weights(read, duos, 4, value_base, rep, value_offset))
    for i, weight in enumerate(key_weights + value_weights):
        wide[i : i + 1, :] = jnp.broadcast_to(weight, (1, features))

    def body(r):
        key_out[r, :] = sum(wide[i : i + 1, :] * key_blocks[i, r, :] for i in range(groups))
        value_out[r, :] = sum(
            wide[groups + i : groups + i + 1, :] * value_full[i, 0, r, :] for i in range(duos)
        )

    over(0, block, body)


def shards(
    tokens, key_cotangent, value_cotangent, key_weight, value_weight, key_moment, value_moment
):
    replicas, shard_count = lax.axis_size("rep"), lax.axis_size("shard")
    depth, width = tokens.shape
    features = key_cotangent.shape[1]
    groups, duos = replicas // 2, replicas // 4
    block = width // replicas
    f32, dma = jnp.float32, pltpu.SemaphoreType.DMA
    entries = groups * (groups + 1) + duos * (duos + 1)
    lines = -(-entries // LANES)

    def small(span, lines=1):
        return [
            pltpu.VMEM((lines, LANES), f32),
            pltpu.VMEM((span * shard_count, lines, LANES), f32),
        ]

    def coded(count):
        return [pltpu.VMEM((max(count, 1), block, features), CODE)] * 2

    def pair(*shape):
        return [dma(shape)] * 2

    parts = min(PARTS, block // 16)
    scratch = [
        pltpu.VMEM((depth, width), tokens.dtype),
        pltpu.VMEM((2, depth, features), key_cotangent.dtype),
        pltpu.VMEM((groups, 2, block, features), f32),
        pltpu.VMEM((groups, 2, block, features), f32),
        pltpu.VMEM((groups, block, features), f32),
        pltpu.VMEM((groups, block, features), f32),
        *coded(groups - 1), *coded(duos), *coded(duos - 1), *coded(2),
        pltpu.VMEM((8, LANES), f32),
        pltpu.VMEM((groups + duos, features), f32),
        pltpu.VMEM((2, 1, LANES), f32), pltpu.VMEM((2, 1, LANES), f32),
        *small(2), *small(2), *small(4), *small(replicas, lines),
        dma((BUNCHES,)), dma((2, SPLITS)), *pair(2, BUNCHES, SPLITS),
        *pair(groups - 1, parts), *pair(duos, parts), *pair(max(duos - 1, 1), parts),
        *pair(2), *pair(2),
        *pair(2 * shard_count), *pair(2 * shard_count), *pair(4 * shard_count),
        *pair(replicas * shard_count),
    ]
    key_merged, value_merged = pl.pallas_call(
        functools.partial(merge_kernel, replicas, shard_count),
        out_shape=[pltpu.VMEM((block, features), f32)] * 2,
        in_specs=[pl.BlockSpec(memory_space=pl.ANY)] * 3,
        out_specs=[pl.BlockSpec(memory_space=pltpu.VMEM)] * 2,
        scratch_shapes=scratch,
        compiler_params=pltpu.CompilerParams(
            collective_id=0, has_side_effects=True, vmem_limit_bytes=VMEM_LIMIT
        ),
    )(tokens, key_cotangent, value_cotangent)
    new_key_moment = MOMENTUM_DECAY * key_moment + key_merged
    new_value_moment = MOMENTUM_DECAY * value_moment + value_merged
    new_key_weight = key_weight - STEP_SIZE * new_key_moment
    new_value_weight = value_weight - STEP_SIZE * new_value_moment
    return new_key_weight, new_value_weight, new_key_moment, new_value_moment


def solution(mesh):
    grads = (P("rep", None),) * 2
    rows = (P(("shard", "rep"), None),) * 4
    return jax.shard_map(
        shards, mesh=mesh, in_specs=(P("rep", "shard"),) + grads + rows, out_specs=rows,
        check_vma=False,
    )
```

```python
import functools
import math

import jax
import jax.numpy as jnp
from jax import lax
from jax.experimental import pallas as pl
from jax.experimental.pallas import tpu as pltpu
from jax.sharding import PartitionSpec as P

EPSILON = 1e-06
MOMENTUM_DECAY = 0.9
STEP_SIZE = 0.01
TINY_BOUND = 1e-16
TOP = 32768.0
FLOOR = 2.0**-120
CODE = jnp.bfloat16
MESH = pl.DeviceIdType.MESH
LANES = 128
ROWS = 32
PARTS = 4
BUNCHES = 4
SPLITS = 2
EARLY = 1
BEHIND = 3
RAW = 2
RAW_PARTS = 3
VMEM_LIMIT = 54 * 2**20


def pair_coefs(cross, first_square, second_square):
    first = 1.0 - cross / (2.0 * (first_square + EPSILON))
    second = 1.0 - cross / (2.0 * (second_square + EPSILON))
    return first, second


def tree_coefs(gram):
    count = len(gram)
    coefs = [1.0] * count
    span = 1
    while len(gram) > 1:
        pairs = [
            pair_coefs(gram[i][i + 1], gram[i][i], gram[i + 1][i + 1])
            for i in range(0, len(gram), 2)
        ]
        for member in range(count):
            coefs[member] = coefs[member] * pairs[member // (2 * span)][member // span % 2]
        half = len(gram) // 2
        merged = [[None] * half for _ in range(half)]
        for i in range(half):
            for j in range(half):
                merged[i][j] = sum(
                    pairs[i][a] * pairs[j][b] * gram[2 * i + a][2 * j + b]
                    for a in range(2)
                    for b in range(2)
                )
        gram = merged
        span *= 2
    return coefs


def norm_bound(coefs, squares):
    bound = jnp.abs(coefs[0]) * jnp.sqrt(squares[0]) + jnp.abs(coefs[1]) * jnp.sqrt(squares[1])
    return jnp.maximum(bound, TINY_BOUND)


def sided(is_first, own, other):
    return jnp.where(is_first, own, other), jnp.where(is_first, other, own)


def encode(value):
    power = value * value
    power = power * power
    power = power * power
    return jnp.where(value < 0.0, -power, power).astype(CODE)


def decode(coded):
    coded = coded.astype(jnp.float32)
    fourth = lax.rsqrt(lax.rsqrt(jnp.maximum(jnp.abs(coded), FLOOR)))
    eighth = fourth * lax.rsqrt(fourth)
    return jnp.where(coded > 0.0, eighth, jnp.where(coded < 0.0, -eighth, 0.0))


def tree_sum(terms):
    while len(terms) > 1:
        terms = [sum(terms[i : i + 2]) for i in range(0, len(terms), 2)]
    return terms[0]


def fold(product):
    return tree_sum([
        product[i : i + 8, j : j + LANES]
        for i in range(0, product.shape[0], 8)
        for j in range(0, product.shape[1], LANES)
    ])


def scalar(tile):
    return jnp.sum(jnp.sum(tile, axis=0, keepdims=True), axis=1, keepdims=True)


def wrapped(position, shift, size):
    moved = position + shift
    return jnp.where(moved >= size, moved - size, moved)


class Exchange:
    def __init__(self, span, shard_count, rep, shard, payload, inbox, send_sem, recv_sem):
        self.span, self.shard_count, self.rep, self.shard = span, shard_count, rep, shard
        self.payload, self.inbox = payload, inbox
        self.send_sem, self.recv_sem = send_sem, recv_sem
        self.shape = payload.shape

    def start(self, placed):
        flat = lax.broadcasted_iota(jnp.int32, self.shape, 0) * LANES
        flat = flat + lax.broadcasted_iota(jnp.int32, self.shape, 1)
        tiles = [jnp.where(flat == place, value, 0.0) for place, value in placed]
        self.payload[...] = tree_sum(tiles)
        inside = lax.rem(self.rep, self.span)
        nears = [self.rep - inside + wrapped(inside, i, self.span) for i in range(self.span)]
        fars = [wrapped(self.shard, i, self.shard_count) for i in range(self.shard_count)]
        for near in sorted(range(self.span), key=lambda n: -min(n, self.span - n)):
            for far in reversed(range(self.shard_count)):
                if near or far:
                    pltpu.make_async_remote_copy(
                        src_ref=self.payload,
                        dst_ref=self.inbox.at[far * self.span + near - 1],
                        send_sem=self.send_sem,
                        recv_sem=self.recv_sem,
                        device_id=(fars[far], nears[near]),
                        device_id_type=MESH,
                    ).start()

    def all_copies(self, sem):
        return pltpu.make_async_copy(self.inbox, self.inbox, sem)

    def finish(self):
        self.all_copies(self.recv_sem).wait()
        count = self.span * self.shard_count - 1
        total = tree_sum([self.payload[...]] + [self.inbox[slot] for slot in range(count)])

        def read(place):
            line, lane = place // LANES, place % LANES
            row = total[line : line + 1, :]
            return (pltpu.roll(row, LANES - lane, 1) if lane else row)[:, :1]

        return read

    def drain(self):
        self.all_copies(self.send_sem).wait()


def owns(rep, shard, members):
    return (shard == 0) & (lax.rem(rep, members) == 0)


def final_places(sums, count, size, base, scale, rep, shard, offset):
    unit = lax.div(rep, size)
    for (i, j), value in sums:
        left = lax.rem(unit - offset(i) + count, count)
        right = lax.rem(unit - offset(j) + count, count)
        yield base + jnp.minimum(left, right) * count + jnp.maximum(left, right), value
    yield base + count * count + unit, jnp.where(owns(rep, shard, size), scale, 0.0)


def final_weights(read, count, size, base, rep, offset):
    unit = lax.div(rep, size)
    scales = [read(base + count * count + i) for i in range(count)]
    gram = [[None] * count for _ in range(count)]
    for i in range(count):
        for j in range(i, count):
            gram[i][j] = read(base + i * count + j) * (scales[i] * scales[j])
            gram[j][i] = gram[i][j]
    weights = [coef * scale for coef, scale in zip(tree_coefs(gram), scales)]
    for slot in range(count):
        source = lax.rem(unit - offset(slot) + count, count)
        chosen = weights[0]
        for i in range(1, count):
            chosen = jnp.where(source == i, weights[i], chosen)
        yield chosen


def merge_kernel(replicas, shard_count, *refs):
    tokens_hbm, key_hbm, value_hbm = refs[:3]
    key_out, value_out = refs[3:5]
    (
        tokens, cotangents, key_full, value_full, key_other, value_other,
        key_send, key_recv, half_send, half_recv, last_send, last_recv, raw_send, raw_recv,
        held, wide, raw_pay, raw_in,
        key_pay, key_in, value_pay, value_in, duo_pay, duo_in, final_pay, final_in,
        token_sem, load_sem, swap_send, swap_recv,
        key_ss, key_rs, half_ss, half_rs, last_ss, last_rs, raw_ss, raw_rs, rw_s, rw_r,
        kx_s, kx_r, vx_s, vx_r, dx_s, dx_r, fx_s, fx_r,
    ) = refs[5:]
    rep, shard = lax.axis_index("rep"), lax.axis_index("shard")
    groups, duos = replicas // 2, replicas // 4
    core, group = lax.rem(rep, 2), lax.div(rep, 2)
    half, duo = lax.rem(group, 2), lax.div(group, 2)
    block, features = key_other.shape[1], key_other.shape[2]
    width = features // SPLITS
    factor = 1.0 / math.sqrt(tokens.shape[0])
    size = min(block, ROWS)
    parts = min(PARTS, block // 16)
    part = block // parts
    raw_parts = min(RAW_PARTS, parts)
    raw_rows = raw_parts * part
    barrier = pltpu.get_barrier_semaphore()

    forward = group < duos
    inner = (half == 1) == forward
    outer = jnp.logical_not(inner)

    def key_shift(step):
        return jnp.where(forward, step, groups - step)

    raw_target = lax.rem(group + key_shift(RAW), groups)
    before = lax.rem(group + groups - RAW, groups)
    after = lax.rem(group + RAW, groups)
    raw_before = (before < duos) & (lax.rem(before, 2) == 1)
    raw_after = (after >= duos) & (lax.rem(after, 2) == 0)
    receiver = raw_before | raw_after
    plain = jnp.logical_not(receiver)

    bunch = groups // BUNCHES
    span = 2 * block * bunch

    def token_copy(j):
        columns = pl.ds(pl.multiple_of(j * span, span), span)
        return pltpu.make_async_copy(
            tokens_hbm.at[:, columns], tokens.at[:, columns], token_sem.at[j]
        )

    def load(which, split):
        source = key_hbm if which == 0 else value_hbm
        columns = pl.ds(split * width, width)
        return pltpu.make_async_copy(
            source.at[:, columns], cotangents.at[which, :, columns], load_sem.at[which, split]
        )

    first = jnp.where(inner, lax.div(raw_target, bunch), 0)

    def order(k):
        return lax.rem(first + k, BUNCHES)

    token_copy(order(0)).start()
    for split in range(SPLITS):
        load(0, split).start()

    nears = [wrapped(rep, i, replicas) for i in range(replicas)]
    fars = [wrapped(shard, i, shard_count) for i in range(shard_count)]
    for near in range(replicas):
        for far in range(shard_count):
            if near or far:
                pl.semaphore_signal(
                    barrier, inc=1, device_id=(fars[far], nears[near]), device_id_type=MESH
                )

    def remote(source, target, send_sem, recv_sem, peer):
        return pltpu.make_async_remote_copy(
            src_ref=source, dst_ref=target, send_sem=send_sem, recv_sem=recv_sem,
            device_id=(shard, peer), device_id_type=MESH,
        )

    def tensor(which):
        return (key_full, key_other) if which == 0 else (value_full, value_other)

    def place(split):
        return pl.ds(split * width, width)

    def swap(which, at, split):
        full, other = tensor(which)
        these = pl.ds(at * bunch, bunch)
        return remote(
            full.at[these, 1 - core, :, place(split)], other.at[these, :, place(split)],
            swap_send.at[which, at, split], swap_recv.at[which, at, split], rep + 1 - 2 * core,
        )

    def multiply(which, at, split):
        full = tensor(which)[0]
        left = tokens[:, pl.ds(pl.multiple_of(at * span, span), span)]
        product = lax.dot_general(
            left, cotangents[which, :, place(split)], (((0,), (0,)), ((), ())),
            preferred_element_type=jnp.float32,
        ) * factor
        for j in range(bunch):
            for side in range(2):
                begin = (2 * j + side) * block
                full[at * bunch + j, side, :, place(split)] = product[begin : begin + block]

    def duel(left, right, sums):
        products = (left * right, left * left, right * right)
        return tuple(s + fold(p) for s, p in zip(sums, products))

    def swapped(which, at, split, sums):
        full, other = tensor(which)
        for j in range(bunch):
            sums = duel(
                full[at * bunch + j, core, :, place(split)], other[at * bunch + j, :, place(split)],
                sums,
            )
        return sums

    def rows(i, size=size):
        return pl.ds(pl.multiple_of(i * size, size), size)

    def over(begin, length, body, start=None):
        if start is None:
            lax.fori_loop(begin // size, (begin + length) // size, lambda i, _: body(rows(i)), None)
            return None
        return lax.fori_loop(
            begin // size, (begin + length) // size, lambda i, c: body(rows(i), c), start
        )

    zero = jnp.zeros((8, LANES), jnp.float32)

    def pair_sums(which, sums):
        for split in range(SPLITS):
            swap(which, order(BUNCHES - 1), split).wait_recv()
            sums = swapped(which, order(BUNCHES - 1), split, sums)
        return [scalar(tile) for tile in sums]

    def pair_places(sums, is_first):
        first, second = sided(is_first, sums[1], sums[2])
        return [(0, sums[0]), (1, first), (2, second)]

    def pair_finish(read):
        squares = (read(1), read(2))
        first, second = pair_coefs(read(0), *squares)
        scale = norm_bound((first, second), squares) / TOP
        own, other = sided(core == 0, first / scale, second / scale)
        return own, other, scale

    def hold(at, values):
        for i, value in enumerate(values):
            held[at + i : at + i + 1, :] = jnp.broadcast_to(value, (1, LANES))

    def holds(at, count):
        return [held[at + i : at + i + 1, 0:1] for i in range(count)]

    def around(span, *scratch):
        return Exchange(span, shard_count, rep, shard, *scratch)

    key_exchange = around(2, key_pay, key_in, kx_s, kx_r)
    value_exchange = around(2, value_pay, value_in, vx_s, vx_r)
    duo_exchange = around(4, duo_pay, duo_in, dx_s, dx_r)
    final_exchange = around(replicas, final_pay, final_in, fx_s, fx_r)

    def key_copy(step, q):
        shift = key_shift(step)
        place = pl.ds(q * part, part)
        return remote(
            key_send.at[shift - 1, place], key_recv.at[shift - 1, place],
            key_ss.at[shift - 1, q], key_rs.at[shift - 1, q],
            2 * lax.rem(group + shift, groups) + core,
        )

    def key_start(step, begin=0, end=parts):
        for q in range(begin, min(end, parts)):
            key_copy(step, q).start()

    def key_encode(step, q=None):
        own, other = holds(0, 2)
        shift = key_shift(step)
        target = lax.rem(group + shift, groups)

        def body(r):
            key_send[shift - 1, r, :] = encode(
                own * key_full[target, core, r, :] + other * key_other[target, r, :]
            )

        over(0 if q is None else q * part, block if q is None else part, body)

    def half_copy(d, q):
        place = pl.ds(q * part, part)
        return remote(
            half_send.at[d, place], half_recv.at[d, place], half_ss.at[d, q], half_rs.at[d, q],
            rep + 2 - 4 * half,
        )

    def last_copy(step, q):
        place = pl.ds(q * part, part)
        target = lax.rem(duo + step, duos)
        return remote(
            last_send.at[step - 1, place], last_recv.at[step - 1, place],
            last_ss.at[step - 1, q], last_rs.at[step - 1, q], rep + 4 * (target - duo),
        )

    far, near = groups - 1, 1
    middle = list(range(groups - 2, 1, -1))
    mixed = [step for step in middle if step != RAW]

    def advance(which, k, sums):
        for split in range(SPLITS):
            swap(which, order(k - 1), split).wait_recv()
            sums = swapped(which, order(k - 1), split, sums)
            multiply(which, order(k), split)
            swap(which, order(k), split).start()
        return sums

    token_copy(order(0)).wait()
    for split in range(SPLITS):
        load(0, split).wait()
        if split == 0:
            token_copy(order(1)).start()
        multiply(0, order(0), split)

    def raw_copy(side):
        these = pl.ds(0, raw_rows)
        return remote(
            raw_send.at[side, these], raw_recv.at[core, these], raw_ss.at[side], raw_rs.at[core],
            2 * raw_target + side,
        )

    def raw_weight(side):
        return remote(
            raw_pay.at[side], raw_in.at[core], rw_s.at[side], rw_r.at[core],
            2 * raw_target + side,
        )

    @pl.when(inner)
    def _():
        for side in range(2):
            def body(r, carry, side=side):
                value = key_full[raw_target, side, r, :]
                return carry + fold(value * value)

            square = scalar(over(0, raw_rows, body, zero))
            scale = jnp.maximum(jnp.sqrt(square), TINY_BOUND) / TOP
            hold(6 + side, [scale])
            inverse = 1.0 / scale

            def body(r, side=side):
                raw_send[side, r, :] = encode(inverse * key_full[raw_target, side, r, :])

            over(0, raw_rows, body)

    pl.semaphore_wait(barrier, replicas * shard_count - 1)
    for split in range(SPLITS):
        swap(0, order(0), split).start()

    @pl.when(inner)
    def _():
        for side in range(2):
            raw_copy(side).start()

    def body(k, sums):
        token_copy(order(k)).wait()

        @pl.when(k < BUNCHES - 1)
        def _():
            token_copy(order(k + 1)).start()

        @pl.when(k == BUNCHES - 1)
        def _():
            for split in range(SPLITS):
                load(1, split).start()

        return advance(0, k, sums)

    sums = lax.fori_loop(1, BUNCHES, body, (zero,) * 3)
    key_exchange.start(pair_places(pair_sums(0, sums), core == 0))
    for split in range(SPLITS):
        load(1, split).wait()
    for split in range(SPLITS):
        multiply(1, order(0), split)
        swap(1, order(0), split).start()

    hold(0, pair_finish(key_exchange.finish()))

    @pl.when(outer)
    def _():
        for q in range(parts):
            key_encode(far, q)
            key_start(far, q, q + 1)

    @pl.when(inner)
    def _():
        own = holds(0, 1)[0]
        for side in range(2):
            weight = own * holds(6 + side, 1)[0]
            raw_pay[side] = jnp.broadcast_to(weight, (1, LANES))
            raw_weight(side).start()
        for q in range(raw_parts, parts):
            key_encode(RAW, q)
        key_start(RAW, raw_parts)
        key_encode(near)
        key_start(near)

    sums = lax.fori_loop(1, BUNCHES, lambda at, sums: advance(1, at, sums), (zero,) * 3)
    value_exchange.start(pair_places(pair_sums(1, sums), core == 0))

    @pl.when(outer)
    def _():
        for step in middle:
            key_encode(step)
            key_start(step, 0, EARLY)
        key_encode(near)

    @pl.when(inner)
    def _():
        for step in mixed:
            key_encode(step)
            key_start(step, 0, EARLY)
        key_encode(far)


    own, other, value_scale = pair_finish(value_exchange.finish())
    hold(3, (own, other, value_scale))

    def half_block(r, d, side):
        j = 2 * d + side
        return own * value_full[j, core, r, :] + other * value_other[j, r, :]

    for d in range(duos):
        for q in range(parts):
            def body(r):
                half_send[d, r, :] = encode(half_block(r, d, 1 - half))

            over(q * part, part, body)
            half_copy(d, q).start()

    @pl.when(outer)
    def _():
        for step in middle:
            key_start(step, EARLY, BEHIND)

    for d in range(duos):
        def body(r):
            value_other[2 * d + half, r, :] = half_block(r, d, half)

        over(0, block, body)

    key_blocks = key_other
    own, other, key_scale = holds(0, 3)

    def body(r, carry):
        value = own * key_full[group, core, r, :] + other * key_other[group, r, :]
        key_blocks[0, r, :] = value
        return carry + fold(value * value)

    key_sums, value_sums = {(0, 0): over(0, block, body, zero)}, {}
    key_ready, value_ready = [0], []

    def absorb(read, blocks, slot, ready, sums, begin, length):
        def body(r, carry):
            value = read(r)
            blocks(slot, r, value)
            others = [blocks(b, r) for b in ready] + [value]
            return tuple(c + fold(value * o) for c, o in zip(carry, others))

        pairs = [(b, slot) for b in ready] + [(slot, slot)]
        start = tuple(sums.get(pair, zero) for pair in pairs)
        sums.update(zip(pairs, over(begin, length, body, start)))

    def key_access(slot, r, value=None):
        if value is None:
            return key_blocks[slot, r, :]
        key_blocks[slot, r, :] = value

    def value_access(slot, r, value=None):
        if value is None:
            return value_full[slot, 0, r, :]
        value_full[slot, 0, r, :] = value

    def key_offset(u):
        return jnp.where(half == 0, u, lax.rem(groups - u, groups))

    def value_offset(u):
        return u

    def key_arrival(u, q):
        shift, place = key_offset(u), pl.ds(q * part, part)
        remote(
            key_send.at[shift - 1, place], key_recv.at[shift - 1, place],
            key_ss.at[shift - 1, q], key_rs.at[shift - 1, q], rep + 1 - 2 * core,
        ).wait_recv()

    def absorb_key(u, q):
        key_arrival(u, q)
        absorb(
            lambda r: decode(key_recv[key_offset(u) - 1, r, :]), key_access, u, key_ready,
            key_sums, q * part, part,
        )

    @pl.when(receiver)
    def _():
        for source in range(2):
            these = pl.ds(0, raw_rows)
            remote(
                raw_send.at[source, these], raw_recv.at[source, these], raw_ss.at[source],
                raw_rs.at[source], rep + 1 - 2 * core,
            ).wait_recv()
            remote(
                raw_pay.at[source], raw_in.at[source], rw_s.at[source], rw_r.at[source],
                rep + 1 - 2 * core,
            ).wait_recv()

        def body(r):
            key_blocks[groups - RAW, r, :] = sum(
                raw_in[source][:, :1] * decode(raw_recv[source, r, :]) for source in range(2)
            )

        over(0, raw_rows, body)

    for q in range(parts):
        absorb_key(1, q)
    key_ready.append(1)

    duo_sums = (zero,) * 3
    for d in range(duos):
        for q in range(parts):
            half_copy(d, q).wait_recv()

            def body(r, carry):
                left = value_other[2 * d + half, r, :]
                right = decode(half_recv[d, r, :])
                value_other[2 * d + 1 - half, r, :] = right
                return duel(left, right, carry)

            duo_sums = over(q * part, part, body, duo_sums)
    even = half == 0
    places = pair_places([scalar(tile) for tile in duo_sums], even)
    mine = jnp.where(owns(rep, shard, 2), value_scale, 0.0)
    low, high = sided(even, mine, jnp.zeros_like(mine))
    duo_exchange.start(places + [(3, low), (4, high)])

    @pl.when(outer)
    def _():
        for step in middle:
            key_start(step, BEHIND)

    @pl.when(inner)
    def _():
        for step in mixed:
            key_start(step, EARLY)
        key_start(far)

    for at in range(BUNCHES):
        for split in range(SPLITS):
            swap(1, at, split).wait_send()
    read = duo_exchange.finish()
    low, high = read(3), read(4)
    squares = (read(1) * (low * low), read(2) * (high * high))
    first, second = pair_coefs(read(0) * (low * high), *squares)
    duo_scale = norm_bound((first, second), squares) / TOP
    own, other = sided(even, first * low / duo_scale, second * high / duo_scale)

    def duo_block(target, r):
        return (
            own * value_other[2 * target + half, r, :]
            + other * value_other[2 * target + 1 - half, r, :]
        )

    for step in range(1, duos):
        for q in range(parts):
            def body(r):
                last_send[step - 1, r, :] = encode(duo_block(lax.rem(duo + step, duos), r))

            over(q * part, part, body)
            last_copy(step, q).start()

    @pl.when(outer)
    def _():
        key_start(near)

    absorb(lambda r: duo_block(duo, r), value_access, 0, value_ready, value_sums, 0, block)
    value_ready.append(0)
    for u in range(2, groups - 1):
        if u == groups - RAW:
            def unpack(begin, end):
                for q in range(begin, end):
                    key_arrival(u, q)

                    def body(r):
                        key_blocks[u, r, :] = decode(key_recv[key_offset(u) - 1, r, :])

                    over(q * part, part, body)

            pl.when(plain)(lambda: unpack(0, raw_parts))
            unpack(raw_parts, parts)
            absorb(
                lambda r: key_blocks[u, r, :], key_access, u, key_ready, key_sums, 0, block
            )
        else:
            for q in range(parts):
                absorb_key(u, q)
        key_ready.append(u)
    for step in range(1, duos):
        for q in range(parts):
            last_copy(step, q).wait_recv()
            absorb(
                lambda r: decode(last_recv[step - 1, r, :]), value_access, step, value_ready,
                value_sums, q * part, part,
            )
            if step == duos - 1:
                absorb_key(groups - 1, q)
        value_ready.append(step)

    key_base, value_base = 0, groups * (groups + 1)
    key_places = [(pair, scalar(tile)) for pair, tile in key_sums.items()]
    value_places = [(pair, scalar(tile)) for pair, tile in value_sums.items()]
    final_exchange.start(
        list(final_places(key_places, groups, 2, key_base, key_scale, rep, shard, key_offset))
        + list(
            final_places(value_places, duos, 4, value_base, duo_scale, rep, shard, value_offset)
        )
    )
    for at in range(BUNCHES):
        for split in range(SPLITS):
            swap(0, at, split).wait_send()
    for step in range(1, groups):
        def drain(begin, end, step=step):
            for q in range(begin, end):
                key_copy(step, q).wait_send()

        if step == RAW:
            pl.when(outer)(lambda: drain(0, raw_parts))
            drain(raw_parts, parts)
        else:
            drain(0, parts)

    @pl.when(inner)
    def _():
        for side in range(2):
            raw_copy(side).wait_send()
            raw_weight(side).wait_send()

    for q in range(parts):
        for d in range(duos):
            half_copy(d, q).wait_send()
        for step in range(1, duos):
            last_copy(step, q).wait_send()
    for exchange in (key_exchange, value_exchange, duo_exchange):
        exchange.drain()
    read = final_exchange.finish()
    key_weights = list(final_weights(read, groups, 2, key_base, rep, key_offset))
    value_weights = list(final_weights(read, duos, 4, value_base, rep, value_offset))
    for i, weight in enumerate(key_weights + value_weights):
        wide[i : i + 1, :] = jnp.broadcast_to(weight, (1, features))

    def body(r):
        key_out[r, :] = sum(wide[i : i + 1, :] * key_blocks[i, r, :] for i in range(groups))
        value_out[r, :] = sum(
            wide[groups + i : groups + i + 1, :] * value_full[i, 0, r, :] for i in range(duos)
        )

    over(0, block, body)
    final_exchange.drain()


def shards(
    tokens, key_cotangent, value_cotangent, key_weight, value_weight, key_moment, value_moment
):
    replicas, shard_count = lax.axis_size("rep"), lax.axis_size("shard")
    depth, width = tokens.shape
    features = key_cotangent.shape[1]
    groups, duos = replicas // 2, replicas // 4
    block = width // replicas
    f32, dma = jnp.float32, pltpu.SemaphoreType.DMA
    entries = groups * (groups + 1) + duos * (duos + 1)
    lines = -(-entries // LANES)

    def small(span, lines=1):
        return [
            pltpu.VMEM((lines, LANES), f32),
            pltpu.VMEM((span * shard_count - 1, lines, LANES), f32),
        ]

    def coded(count):
        return [pltpu.VMEM((max(count, 1), block, features), CODE)] * 2

    def pair(*shape):
        return [dma(shape)] * 2

    parts = min(PARTS, block // 16)
    scratch = [
        pltpu.VMEM((depth, width), tokens.dtype),
        pltpu.VMEM((2, depth, features), key_cotangent.dtype),
        pltpu.VMEM((groups, 2, block, features), f32),
        pltpu.VMEM((groups, 2, block, features), f32),
        pltpu.VMEM((groups, block, features), f32),
        pltpu.VMEM((groups, block, features), f32),
        *coded(groups - 1), *coded(duos), *coded(duos - 1), *coded(2),
        pltpu.VMEM((8, LANES), f32),
        pltpu.VMEM((groups + duos, features), f32),
        pltpu.VMEM((2, 1, LANES), f32), pltpu.VMEM((2, 1, LANES), f32),
        *small(2), *small(2), *small(4), *small(replicas, lines),
        dma((BUNCHES,)), dma((2, SPLITS)), *pair(2, BUNCHES, SPLITS),
        *pair(groups - 1, parts), *pair(duos, parts), *pair(max(duos - 1, 1), parts),
        *pair(2), *pair(2),
        *[dma] * 8,
    ]
    key_merged, value_merged = pl.pallas_call(
        functools.partial(merge_kernel, replicas, shard_count),
        out_shape=[pltpu.VMEM((block, features), f32)] * 2,
        in_specs=[pl.BlockSpec(memory_space=pl.ANY)] * 3,
        out_specs=[pl.BlockSpec(memory_space=pltpu.VMEM)] * 2,
        scratch_shapes=scratch,
        compiler_params=pltpu.CompilerParams(
            collective_id=0, has_side_effects=True, vmem_limit_bytes=VMEM_LIMIT
        ),
    )(tokens, key_cotangent, value_cotangent)
    new_key_moment = MOMENTUM_DECAY * key_moment + key_merged
    new_value_moment = MOMENTUM_DECAY * value_moment + value_merged
    new_key_weight = key_weight - STEP_SIZE * new_key_moment
    new_value_weight = value_weight - STEP_SIZE * new_value_moment
    return new_key_weight, new_value_weight, new_key_moment, new_value_moment


def solution(mesh):
    grads = (P("rep", None),) * 2
    rows = (P(("shard", "rep"), None),) * 4
    return jax.shard_map(
        shards, mesh=mesh, in_specs=(P("rep", "shard"),) + grads + rows, out_specs=rows,
        check_vma=False,
    )
```

```python
import functools
import math

import jax
import jax.numpy as jnp
from jax import lax
from jax.experimental import pallas as pl
from jax.experimental.pallas import tpu as pltpu
from jax.sharding import PartitionSpec as P

EPSILON = 1e-06
MOMENTUM_DECAY = 0.9
STEP_SIZE = 0.01
TINY_BOUND = 1e-16
TOP = 32768.0
FLOOR = 2.0**-120
CODE = jnp.bfloat16
MESH = pl.DeviceIdType.MESH
LANES = 128
ROWS = 64
PARTS = 4
BUNCHES = 4
SPLITS = 2
EARLY = 1
BEHIND = 4
RAW = 2
RAW_PARTS = 3
VMEM_LIMIT = 54 * 2**20


def pair_coefs(cross, first_square, second_square):
    first = 1.0 - cross / (2.0 * (first_square + EPSILON))
    second = 1.0 - cross / (2.0 * (second_square + EPSILON))
    return first, second


def tree_coefs(gram):
    count = len(gram)
    coefs = [1.0] * count
    span = 1
    while len(gram) > 1:
        pairs = [
            pair_coefs(gram[i][i + 1], gram[i][i], gram[i + 1][i + 1])
            for i in range(0, len(gram), 2)
        ]
        for member in range(count):
            coefs[member] = coefs[member] * pairs[member // (2 * span)][member // span % 2]
        half = len(gram) // 2
        merged = [[None] * half for _ in range(half)]
        for i in range(half):
            for j in range(half):
                merged[i][j] = sum(
                    pairs[i][a] * pairs[j][b] * gram[2 * i + a][2 * j + b]
                    for a in range(2)
                    for b in range(2)
                )
        gram = merged
        span *= 2
    return coefs


def norm_bound(coefs, squares):
    bound = jnp.abs(coefs[0]) * jnp.sqrt(squares[0]) + jnp.abs(coefs[1]) * jnp.sqrt(squares[1])
    return jnp.maximum(bound, TINY_BOUND)


def sided(is_first, own, other):
    return jnp.where(is_first, own, other), jnp.where(is_first, other, own)


def encode(value):
    power = value * value
    power = power * power
    power = power * power
    return jnp.where(value < 0.0, -power, power).astype(CODE)


def decode(coded):
    coded = coded.astype(jnp.float32)
    fourth = lax.rsqrt(lax.rsqrt(jnp.maximum(jnp.abs(coded), FLOOR)))
    eighth = fourth * lax.rsqrt(fourth)
    return jnp.where(coded > 0.0, eighth, jnp.where(coded < 0.0, -eighth, 0.0))


def tree_sum(terms):
    while len(terms) > 1:
        terms = [sum(terms[i : i + 2]) for i in range(0, len(terms), 2)]
    return terms[0]


def fold(product):
    return tree_sum([
        product[i : i + 8, j : j + LANES]
        for i in range(0, product.shape[0], 8)
        for j in range(0, product.shape[1], LANES)
    ])


def scalar(tile):
    return jnp.sum(jnp.sum(tile, axis=0, keepdims=True), axis=1, keepdims=True)


def wrapped(position, shift, size):
    moved = position + shift
    return jnp.where(moved >= size, moved - size, moved)


class Exchange:
    def __init__(self, span, shard_count, rep, shard, payload, inbox, send_sem, recv_sem):
        self.span, self.shard_count, self.rep, self.shard = span, shard_count, rep, shard
        self.payload, self.inbox = payload, inbox
        self.send_sem, self.recv_sem = send_sem, recv_sem
        self.shape = payload.shape

    def start(self, placed):
        flat = lax.broadcasted_iota(jnp.int32, self.shape, 0) * LANES
        flat = flat + lax.broadcasted_iota(jnp.int32, self.shape, 1)
        tiles = [jnp.where(flat == place, value, 0.0) for place, value in placed]
        self.payload[...] = tree_sum(tiles)
        inside = lax.rem(self.rep, self.span)
        nears = [self.rep - inside + wrapped(inside, i, self.span) for i in range(self.span)]
        fars = [wrapped(self.shard, i, self.shard_count) for i in range(self.shard_count)]
        for near in sorted(range(self.span), key=lambda n: -min(n, self.span - n)):
            for far in reversed(range(self.shard_count)):
                if near or far:
                    pltpu.make_async_remote_copy(
                        src_ref=self.payload,
                        dst_ref=self.inbox.at[far * self.span + near - 1],
                        send_sem=self.send_sem,
                        recv_sem=self.recv_sem,
                        device_id=(fars[far], nears[near]),
                        device_id_type=MESH,
                    ).start()

    def all_copies(self, sem):
        return pltpu.make_async_copy(self.inbox, self.inbox, sem)

    def finish(self):
        self.all_copies(self.recv_sem).wait()
        count = self.span * self.shard_count - 1
        total = tree_sum([self.payload[...]] + [self.inbox[slot] for slot in range(count)])

        def read(place):
            line, lane = place // LANES, place % LANES
            row = total[line : line + 1, :]
            return (pltpu.roll(row, LANES - lane, 1) if lane else row)[:, :1]

        return read

    def drain(self):
        self.all_copies(self.send_sem).wait()


def owns(rep, shard, members):
    return (shard == 0) & (lax.rem(rep, members) == 0)


def final_places(sums, count, size, base, scale, rep, shard, offset):
    unit = lax.div(rep, size)
    for (i, j), value in sums:
        left = lax.rem(unit - offset(i) + count, count)
        right = lax.rem(unit - offset(j) + count, count)
        yield base + jnp.minimum(left, right) * count + jnp.maximum(left, right), value
    yield base + count * count + unit, jnp.where(owns(rep, shard, size), scale, 0.0)


def final_weights(read, count, size, base, rep, offset):
    unit = lax.div(rep, size)
    scales = [read(base + count * count + i) for i in range(count)]
    gram = [[None] * count for _ in range(count)]
    for i in range(count):
        for j in range(i, count):
            gram[i][j] = read(base + i * count + j) * (scales[i] * scales[j])
            gram[j][i] = gram[i][j]
    weights = [coef * scale for coef, scale in zip(tree_coefs(gram), scales)]
    for slot in range(count):
        source = lax.rem(unit - offset(slot) + count, count)
        chosen = weights[0]
        for i in range(1, count):
            chosen = jnp.where(source == i, weights[i], chosen)
        yield chosen


def merge_kernel(replicas, shard_count, *refs):
    tokens_hbm, key_hbm, value_hbm = refs[:3]
    key_out, value_out = refs[3:5]
    (
        tokens, cotangents, key_full, value_full, key_other, value_other,
        key_send, key_recv, half_send, half_recv, last_send, last_recv, raw_send, raw_recv,
        held, wide, raw_pay, raw_in,
        key_pay, key_in, value_pay, value_in, duo_pay, duo_in, final_pay, final_in,
        token_sem, load_sem, swap_send, swap_recv,
        key_ss, key_rs, half_ss, half_rs, last_ss, last_rs, raw_ss, raw_rs, rw_s, rw_r,
        kx_s, kx_r, vx_s, vx_r, dx_s, dx_r, fx_s, fx_r,
    ) = refs[5:]
    rep, shard = lax.axis_index("rep"), lax.axis_index("shard")
    groups, duos = replicas // 2, replicas // 4
    core, group = lax.rem(rep, 2), lax.div(rep, 2)
    half, duo = lax.rem(group, 2), lax.div(group, 2)
    block, features = key_other.shape[1], key_other.shape[2]
    width = features // SPLITS
    factor = 1.0 / math.sqrt(tokens.shape[0])
    parts = min(PARTS, block // 16)
    part = block // parts
    size = min(part, ROWS)
    raw_parts = min(RAW_PARTS, parts)
    raw_rows = raw_parts * part
    barrier = pltpu.get_barrier_semaphore()

    forward = group < duos
    inner = (half == 1) == forward
    outer = jnp.logical_not(inner)

    def key_shift(step):
        return jnp.where(forward, step, groups - step)

    raw_target = lax.rem(group + key_shift(RAW), groups)
    before = lax.rem(group + groups - RAW, groups)
    after = lax.rem(group + RAW, groups)
    raw_before = (before < duos) & (lax.rem(before, 2) == 1)
    raw_after = (after >= duos) & (lax.rem(after, 2) == 0)
    receiver = raw_before | raw_after
    plain = jnp.logical_not(receiver)

    bunch = groups // BUNCHES
    span = 2 * block * bunch

    def token_copy(j):
        columns = pl.ds(pl.multiple_of(j * span, span), span)
        return pltpu.make_async_copy(
            tokens_hbm.at[:, columns], tokens.at[:, columns], token_sem.at[j]
        )

    def load(which, split):
        source = key_hbm if which == 0 else value_hbm
        columns = pl.ds(split * width, width)
        return pltpu.make_async_copy(
            source.at[:, columns], cotangents.at[which, :, columns], load_sem.at[which, split]
        )

    first = jnp.where(inner, lax.div(raw_target, bunch), 0)

    def order(k):
        return lax.rem(first + k, BUNCHES)

    token_copy(order(0)).start()
    for split in range(SPLITS):
        load(0, split).start()

    nears = [wrapped(rep, i, replicas) for i in range(replicas)]
    fars = [wrapped(shard, i, shard_count) for i in range(shard_count)]
    for near in range(replicas):
        for far in range(shard_count):
            if near or far:
                pl.semaphore_signal(
                    barrier, inc=1, device_id=(fars[far], nears[near]), device_id_type=MESH
                )

    def remote(source, target, send_sem, recv_sem, peer):
        return pltpu.make_async_remote_copy(
            src_ref=source, dst_ref=target, send_sem=send_sem, recv_sem=recv_sem,
            device_id=(shard, peer), device_id_type=MESH,
        )

    def tensor(which):
        return (key_full, key_other) if which == 0 else (value_full, value_other)

    def place(split):
        return pl.ds(split * width, width)

    def swap(which, at, split):
        full, other = tensor(which)
        these = pl.ds(at * bunch, bunch)
        return remote(
            full.at[these, 1 - core, :, place(split)], other.at[these, :, place(split)],
            swap_send.at[which, at, split], swap_recv.at[which, at, split], rep + 1 - 2 * core,
        )

    def multiply(which, at, split):
        full = tensor(which)[0]
        left = tokens[:, pl.ds(pl.multiple_of(at * span, span), span)]
        product = lax.dot_general(
            left, cotangents[which, :, place(split)], (((0,), (0,)), ((), ())),
            preferred_element_type=jnp.float32,
        ) * factor
        for j in range(bunch):
            for side in range(2):
                begin = (2 * j + side) * block
                full[at * bunch + j, side, :, place(split)] = product[begin : begin + block]

    def duel(left, right, sums):
        products = (left * right, left * left, right * right)
        return tuple(s + fold(p) for s, p in zip(sums, products))

    def swapped(which, at, split, sums):
        full, other = tensor(which)
        for j in range(bunch):
            sums = duel(
                full[at * bunch + j, core, :, place(split)], other[at * bunch + j, :, place(split)],
                sums,
            )
        return sums

    def rows(i, size=size):
        return pl.ds(pl.multiple_of(i * size, size), size)

    def over(begin, length, body, start=None):
        if start is None:
            lax.fori_loop(begin // size, (begin + length) // size, lambda i, _: body(rows(i)), None)
            return None
        return lax.fori_loop(
            begin // size, (begin + length) // size, lambda i, c: body(rows(i), c), start
        )

    zero = jnp.zeros((8, LANES), jnp.float32)

    def pair_sums(which, sums):
        for split in range(SPLITS):
            swap(which, order(BUNCHES - 1), split).wait_recv()
            sums = swapped(which, order(BUNCHES - 1), split, sums)
        return [scalar(tile) for tile in sums]

    def pair_places(sums, is_first):
        first, second = sided(is_first, sums[1], sums[2])
        return [(0, sums[0]), (1, first), (2, second)]

    def pair_finish(read):
        squares = (read(1), read(2))
        first, second = pair_coefs(read(0), *squares)
        scale = norm_bound((first, second), squares) / TOP
        own, other = sided(core == 0, first / scale, second / scale)
        return own, other, scale

    def hold(at, values):
        for i, value in enumerate(values):
            held[at + i : at + i + 1, :] = jnp.broadcast_to(value, (1, LANES))

    def holds(at, count):
        return [held[at + i : at + i + 1, 0:1] for i in range(count)]

    def around(span, *scratch):
        return Exchange(span, shard_count, rep, shard, *scratch)

    key_exchange = around(2, key_pay, key_in, kx_s, kx_r)
    value_exchange = around(2, value_pay, value_in, vx_s, vx_r)
    duo_exchange = around(4, duo_pay, duo_in, dx_s, dx_r)
    final_exchange = around(replicas, final_pay, final_in, fx_s, fx_r)

    def key_copy(step, q):
        shift = key_shift(step)
        place = pl.ds(q * part, part)
        return remote(
            key_send.at[shift - 1, place], key_recv.at[shift - 1, place],
            key_ss.at[shift - 1, q], key_rs.at[shift - 1, q],
            2 * lax.rem(group + shift, groups) + core,
        )

    def key_start(step, begin=0, end=parts):
        for q in range(begin, min(end, parts)):
            key_copy(step, q).start()

    def key_encode(step, q=None):
        own, other = holds(0, 2)
        shift = key_shift(step)
        target = lax.rem(group + shift, groups)

        def body(r):
            key_send[shift - 1, r, :] = encode(
                own * key_full[target, core, r, :] + other * key_other[target, r, :]
            )

        over(0 if q is None else q * part, block if q is None else part, body)

    def half_copy(d, q):
        place = pl.ds(q * part, part)
        return remote(
            half_send.at[d, place], half_recv.at[d, place], half_ss.at[d, q], half_rs.at[d, q],
            rep + 2 - 4 * half,
        )

    def last_copy(step, q):
        place = pl.ds(q * part, part)
        target = lax.rem(duo + step, duos)
        return remote(
            last_send.at[step - 1, place], last_recv.at[step - 1, place],
            last_ss.at[step - 1, q], last_rs.at[step - 1, q], rep + 4 * (target - duo),
        )

    far, near = groups - 1, 1
    middle = list(range(groups - 2, 1, -1))
    mixed = [step for step in middle if step != RAW]

    def advance(which, k, sums):
        for split in range(SPLITS):
            swap(which, order(k - 1), split).wait_recv()
            sums = swapped(which, order(k - 1), split, sums)
            multiply(which, order(k), split)
            swap(which, order(k), split).start()
        return sums

    token_copy(order(0)).wait()
    for split in range(SPLITS):
        load(0, split).wait()
        if split == 0:
            token_copy(order(1)).start()
        multiply(0, order(0), split)

    def raw_copy(side):
        these = pl.ds(0, raw_rows)
        return remote(
            raw_send.at[side, these], raw_recv.at[core, these], raw_ss.at[side], raw_rs.at[core],
            2 * raw_target + side,
        )

    def raw_weight(side):
        return remote(
            raw_pay.at[side], raw_in.at[core], rw_s.at[side], rw_r.at[core],
            2 * raw_target + side,
        )

    @pl.when(inner)
    def _():
        for side in range(2):
            def body(r, carry, side=side):
                value = key_full[raw_target, side, r, :]
                return carry + fold(value * value)

            square = scalar(over(0, raw_rows, body, zero))
            scale = jnp.maximum(jnp.sqrt(square), TINY_BOUND) / TOP
            hold(6 + side, [scale])
            inverse = 1.0 / scale

            def body(r, side=side):
                raw_send[side, r, :] = encode(inverse * key_full[raw_target, side, r, :])

            over(0, raw_rows, body)

    pl.semaphore_wait(barrier, replicas * shard_count - 1)
    for split in range(SPLITS):
        swap(0, order(0), split).start()

    @pl.when(inner)
    def _():
        for side in range(2):
            raw_copy(side).start()

    def body(k, sums):
        token_copy(order(k)).wait()

        @pl.when(k < BUNCHES - 1)
        def _():
            token_copy(order(k + 1)).start()

        @pl.when(k == BUNCHES - 1)
        def _():
            for split in range(SPLITS):
                load(1, split).start()

        return advance(0, k, sums)

    sums = lax.fori_loop(1, BUNCHES, body, (zero,) * 3)
    key_exchange.start(pair_places(pair_sums(0, sums), core == 0))
    for split in range(SPLITS):
        load(1, split).wait()
    for split in range(SPLITS):
        multiply(1, order(0), split)
        swap(1, order(0), split).start()

    hold(0, pair_finish(key_exchange.finish()))

    @pl.when(outer)
    def _():
        for q in range(parts):
            key_encode(far, q)
            key_start(far, q, q + 1)

    @pl.when(inner)
    def _():
        own = holds(0, 1)[0]
        for side in range(2):
            weight = own * holds(6 + side, 1)[0]
            raw_pay[side] = jnp.broadcast_to(weight, (1, LANES))
            raw_weight(side).start()
        for q in range(raw_parts, parts):
            key_encode(RAW, q)
        key_start(RAW, raw_parts)
        key_encode(near)
        key_start(near)

    sums = lax.fori_loop(1, BUNCHES, lambda at, sums: advance(1, at, sums), (zero,) * 3)
    value_exchange.start(pair_places(pair_sums(1, sums), core == 0))

    @pl.when(outer)
    def _():
        for step in middle:
            key_encode(step)
            key_start(step, 0, EARLY)
        key_encode(near)

    @pl.when(inner)
    def _():
        for step in mixed:
            key_encode(step)
            key_start(step, 0, EARLY)
        key_encode(far)


    own, other, value_scale = pair_finish(value_exchange.finish())
    hold(3, (own, other, value_scale))

    def half_block(r, d, side):
        j = 2 * d + side
        return own * value_full[j, core, r, :] + other * value_other[j, r, :]

    for d in range(duos):
        for q in range(parts):
            def body(r):
                half_send[d, r, :] = encode(half_block(r, d, 1 - half))

            over(q * part, part, body)
            half_copy(d, q).start()

    @pl.when(outer)
    def _():
        for step in middle:
            key_start(step, EARLY, BEHIND)

    for d in range(duos):
        def body(r):
            value_other[2 * d + half, r, :] = half_block(r, d, half)

        over(0, block, body)

    key_blocks = key_other
    own, other, key_scale = holds(0, 3)

    def body(r, carry):
        value = own * key_full[group, core, r, :] + other * key_other[group, r, :]
        key_blocks[0, r, :] = value
        return carry + fold(value * value)

    key_sums, value_sums = {(0, 0): over(0, block, body, zero)}, {}
    key_ready, value_ready = [0], []

    def absorb(read, blocks, slot, ready, sums, begin, length):
        def body(r, carry):
            value = read(r)
            blocks(slot, r, value)
            others = [blocks(b, r) for b in ready] + [value]
            return tuple(c + fold(value * o) for c, o in zip(carry, others))

        pairs = [(b, slot) for b in ready] + [(slot, slot)]
        start = tuple(sums.get(pair, zero) for pair in pairs)
        sums.update(zip(pairs, over(begin, length, body, start)))

    def key_access(slot, r, value=None):
        if value is None:
            return key_blocks[slot, r, :]
        key_blocks[slot, r, :] = value

    def value_access(slot, r, value=None):
        if value is None:
            return value_full[slot, 0, r, :]
        value_full[slot, 0, r, :] = value

    def key_offset(u):
        return jnp.where(half == 0, u, lax.rem(groups - u, groups))

    def value_offset(u):
        return u

    def key_arrival(u, q):
        shift, place = key_offset(u), pl.ds(q * part, part)
        remote(
            key_send.at[shift - 1, place], key_recv.at[shift - 1, place],
            key_ss.at[shift - 1, q], key_rs.at[shift - 1, q], rep + 1 - 2 * core,
        ).wait_recv()

    def absorb_key(u, q):
        key_arrival(u, q)
        absorb(
            lambda r: decode(key_recv[key_offset(u) - 1, r, :]), key_access, u, key_ready,
            key_sums, q * part, part,
        )

    @pl.when(receiver)
    def _():
        for source in range(2):
            these = pl.ds(0, raw_rows)
            remote(
                raw_send.at[source, these], raw_recv.at[source, these], raw_ss.at[source],
                raw_rs.at[source], rep + 1 - 2 * core,
            ).wait_recv()
            remote(
                raw_pay.at[source], raw_in.at[source], rw_s.at[source], rw_r.at[source],
                rep + 1 - 2 * core,
            ).wait_recv()

        def body(r):
            key_blocks[groups - RAW, r, :] = sum(
                raw_in[source][:, :1] * decode(raw_recv[source, r, :]) for source in range(2)
            )

        over(0, raw_rows, body)

    for q in range(parts):
        absorb_key(1, q)
    key_ready.append(1)

    duo_sums = (zero,) * 3
    for d in range(duos):
        for q in range(parts):
            half_copy(d, q).wait_recv()

            def body(r, carry):
                left = value_other[2 * d + half, r, :]
                right = decode(half_recv[d, r, :])
                value_other[2 * d + 1 - half, r, :] = right
                return duel(left, right, carry)

            duo_sums = over(q * part, part, body, duo_sums)
    even = half == 0
    places = pair_places([scalar(tile) for tile in duo_sums], even)
    mine = jnp.where(owns(rep, shard, 2), value_scale, 0.0)
    low, high = sided(even, mine, jnp.zeros_like(mine))
    duo_exchange.start(places + [(3, low), (4, high)])

    @pl.when(outer)
    def _():
        for step in middle:
            key_start(step, BEHIND)

    @pl.when(inner)
    def _():
        for step in mixed:
            key_start(step, EARLY)
        key_start(far)

    for at in range(BUNCHES):
        for split in range(SPLITS):
            swap(1, at, split).wait_send()
    read = duo_exchange.finish()
    low, high = read(3), read(4)
    squares = (read(1) * (low * low), read(2) * (high * high))
    first, second = pair_coefs(read(0) * (low * high), *squares)
    duo_scale = norm_bound((first, second), squares) / TOP
    own, other = sided(even, first * low / duo_scale, second * high / duo_scale)

    def duo_block(target, r):
        return (
            own * value_other[2 * target + half, r, :]
            + other * value_other[2 * target + 1 - half, r, :]
        )

    for step in range(1, duos):
        for q in range(parts):
            def body(r):
                last_send[step - 1, r, :] = encode(duo_block(lax.rem(duo + step, duos), r))

            over(q * part, part, body)
            last_copy(step, q).start()

    @pl.when(outer)
    def _():
        key_start(near)

    absorb(lambda r: duo_block(duo, r), value_access, 0, value_ready, value_sums, 0, block)
    value_ready.append(0)
    for u in range(2, groups - 1):
        if u == groups - RAW:
            def unpack(begin, end):
                for q in range(begin, end):
                    key_arrival(u, q)

                    def body(r):
                        key_blocks[u, r, :] = decode(key_recv[key_offset(u) - 1, r, :])

                    over(q * part, part, body)

            pl.when(plain)(lambda: unpack(0, raw_parts))
            unpack(raw_parts, parts)
            absorb(
                lambda r: key_blocks[u, r, :], key_access, u, key_ready, key_sums, 0, block
            )
        else:
            for q in range(parts):
                absorb_key(u, q)
        key_ready.append(u)
    for step in range(1, duos):
        for q in range(parts):
            last_copy(step, q).wait_recv()
            absorb(
                lambda r: decode(last_recv[step - 1, r, :]), value_access, step, value_ready,
                value_sums, q * part, part,
            )
            if step == duos - 1:
                absorb_key(groups - 1, q)
        value_ready.append(step)

    key_base, value_base = 0, groups * (groups + 1)
    key_places = [(pair, scalar(tile)) for pair, tile in key_sums.items()]
    value_places = [(pair, scalar(tile)) for pair, tile in value_sums.items()]
    final_exchange.start(
        list(final_places(key_places, groups, 2, key_base, key_scale, rep, shard, key_offset))
        + list(
            final_places(value_places, duos, 4, value_base, duo_scale, rep, shard, value_offset)
        )
    )
    for at in range(BUNCHES):
        for split in range(SPLITS):
            swap(0, at, split).wait_send()
    for step in range(1, groups):
        def drain(begin, end, step=step):
            for q in range(begin, end):
                key_copy(step, q).wait_send()

        if step == RAW:
            pl.when(outer)(lambda: drain(0, raw_parts))
            drain(raw_parts, parts)
        else:
            drain(0, parts)

    @pl.when(inner)
    def _():
        for side in range(2):
            raw_copy(side).wait_send()
            raw_weight(side).wait_send()

    for q in range(parts):
        for d in range(duos):
            half_copy(d, q).wait_send()
        for step in range(1, duos):
            last_copy(step, q).wait_send()
    for exchange in (key_exchange, value_exchange, duo_exchange):
        exchange.drain()
    read = final_exchange.finish()
    key_weights = list(final_weights(read, groups, 2, key_base, rep, key_offset))
    value_weights = list(final_weights(read, duos, 4, value_base, rep, value_offset))
    for i, weight in enumerate(key_weights + value_weights):
        wide[i : i + 1, :] = jnp.broadcast_to(weight, (1, features))

    def body(r):
        key_out[r, :] = sum(wide[i : i + 1, :] * key_blocks[i, r, :] for i in range(groups))
        value_out[r, :] = sum(
            wide[groups + i : groups + i + 1, :] * value_full[i, 0, r, :] for i in range(duos)
        )

    over(0, block, body)
    final_exchange.drain()


def shards(
    tokens, key_cotangent, value_cotangent, key_weight, value_weight, key_moment, value_moment
):
    replicas, shard_count = lax.axis_size("rep"), lax.axis_size("shard")
    depth, width = tokens.shape
    features = key_cotangent.shape[1]
    groups, duos = replicas // 2, replicas // 4
    block = width // replicas
    f32, dma = jnp.float32, pltpu.SemaphoreType.DMA
    entries = groups * (groups + 1) + duos * (duos + 1)
    lines = -(-entries // LANES)

    def small(span, lines=1):
        return [
            pltpu.VMEM((lines, LANES), f32),
            pltpu.VMEM((span * shard_count - 1, lines, LANES), f32),
        ]

    def coded(count):
        return [pltpu.VMEM((max(count, 1), block, features), CODE)] * 2

    def pair(*shape):
        return [dma(shape)] * 2

    parts = min(PARTS, block // 16)
    scratch = [
        pltpu.VMEM((depth, width), tokens.dtype),
        pltpu.VMEM((2, depth, features), key_cotangent.dtype),
        pltpu.VMEM((groups, 2, block, features), f32),
        pltpu.VMEM((groups, 2, block, features), f32),
        pltpu.VMEM((groups, block, features), f32),
        pltpu.VMEM((groups, block, features), f32),
        *coded(groups - 1), *coded(duos), *coded(duos - 1), *coded(2),
        pltpu.VMEM((8, LANES), f32),
        pltpu.VMEM((groups + duos, features), f32),
        pltpu.VMEM((2, 1, LANES), f32), pltpu.VMEM((2, 1, LANES), f32),
        *small(2), *small(2), *small(4), *small(replicas, lines),
        dma((BUNCHES,)), dma((2, SPLITS)), *pair(2, BUNCHES, SPLITS),
        *pair(groups - 1, parts), *pair(duos, parts), *pair(max(duos - 1, 1), parts),
        *pair(2), *pair(2),
        *[dma] * 8,
    ]
    key_merged, value_merged = pl.pallas_call(
        functools.partial(merge_kernel, replicas, shard_count),
        out_shape=[pltpu.VMEM((block, features), f32)] * 2,
        in_specs=[pl.BlockSpec(memory_space=pl.ANY)] * 3,
        out_specs=[pl.BlockSpec(memory_space=pltpu.VMEM)] * 2,
        scratch_shapes=scratch,
        compiler_params=pltpu.CompilerParams(
            collective_id=0, has_side_effects=True, vmem_limit_bytes=VMEM_LIMIT
        ),
    )(tokens, key_cotangent, value_cotangent)
    new_key_moment = MOMENTUM_DECAY * key_moment + key_merged
    new_value_moment = MOMENTUM_DECAY * value_moment + value_merged
    new_key_weight = key_weight - STEP_SIZE * new_key_moment
    new_value_weight = value_weight - STEP_SIZE * new_value_moment
    return new_key_weight, new_value_weight, new_key_moment, new_value_moment


def solution(mesh):
    grads = (P("rep", None),) * 2
    rows = (P(("shard", "rep"), None),) * 4
    return jax.shard_map(
        shards, mesh=mesh, in_specs=(P("rep", "shard"),) + grads + rows, out_specs=rows,
        check_vma=False,
    )
```
